512 devices in a mesh: view: 16 (over z_lo, y), tile: 32 (over x, z_hi, core).
Axes of the slice: x: 4, y: 4, z: 16 (z_hi: 4, z_lo: 4; z = z_hi * 4 + z_lo), core: 2. Of those that a mesh axis runs over, the one named last changes fastest.
Arguments:
- estimate: float32 [256, 256, 128], P('tile', 'view'), may hold values from 0.5 to 1.5
- images: float32 [16, 256, 256, 128], P('view', 'tile'), may hold values from 0.25 to 4
- taps_first: float32 [16, 5], P('view'), may hold values from 0.1 to 1
- taps_second: float32 [16, 7], P('view'), may hold values from 0.1 to 1
- taps_axial: float32 [16, 33], P('view'), may hold values from 0.02 to 0.2
Outputs:
- deconvolved: float32 [256, 256, 128], P('tile', 'view')
The draws below stay inside these ranges and needn't reach their ends.
All inputs are finite; a program needn't handle non-finite values.
Results may differ from the reference program's by a relative error of at most 0.0001.
Values sent between devices are 32-bit elements; how exact they have to be, the bound alone decides.
No kernel may reach another device: no remote copies, remote signals or barrier semaphores. Data moves between devices by JAX's collectives and lax.ppermute only.
A program may use at most 64 MiB of HBM per device.

```python
import math
import jax
import jax.numpy as jnp
from jax import lax

NY = 256
NZ = 128
RX = 2
RY = 3
RZ = 16
ITERS = 2
VIEWS = 16
NX = 256


def level_of(rng, dims, split, smallest, largest):
    gain = 1.0
    for dim, shards_of in split:
        draws = jax.random.uniform(jax.random.fold_in(jax.random.fold_in(rng, 6), dim), (shards_of,), jnp.float32, smallest / len(split), largest / len(split))
        gain = gain * jnp.repeat(jnp.exp(draws), dims[dim] // shards_of).reshape((-1,) + (1,) * (len(dims) - 1 - dim))
    return gain


def setup_inputs(seed: int = 0) -> dict:
    streams_of = jax.random.split(jax.random.key(seed), 6)
    return {
        "estimate": jnp.clip(0.5 + 1.0 * jax.random.uniform(streams_of[0], (NX, NY, NZ), jnp.float32) ** level_of(streams_of[0], (NX, NY, NZ), ((0, 32), (1, 16)), -0.2, 0.2), 0.5, 1.5),
        "images": jnp.clip(jnp.exp(math.log(4.0) - 2.7725887 * jax.random.uniform(streams_of[1], (VIEWS, NX, NY, NZ), jnp.float32) ** level_of(streams_of[1], (VIEWS, NX, NY, NZ), ((0, 16), (1, 32)), -0.2, 0.2)), 0.25, 4.0),
        "taps_first": jnp.clip(jnp.exp(math.log(1.0) - 2.3025851 * jax.random.uniform(streams_of[2], (VIEWS, 2 * RX + 1), jnp.float32) ** level_of(streams_of[2], (VIEWS, 2 * RX + 1), ((0, 16),), -0.2, 0.2)), 0.1, 1.0),
        "taps_second": jnp.clip(jnp.exp(math.log(1.0) - 2.3025851 * jax.random.uniform(streams_of[3], (VIEWS, 2 * RY + 1), jnp.float32) ** level_of(streams_of[3], (VIEWS, 2 * RY + 1), ((0, 16),), -0.2, 0.2)), 0.1, 1.0),
        "taps_axial": jnp.clip(jnp.exp(math.log(0.2) - 2.3025851 * jax.random.uniform(streams_of[4], (VIEWS, 2 * RZ + 1), jnp.float32) ** level_of(streams_of[4], (VIEWS, 2 * RZ + 1), ((0, 16),), -0.2, 0.2)), 0.02, 0.2),
    }


def toeplitz(taps, length, radius):
    index = jnp.arange(length, dtype=jnp.int32)
    offset = index[None, :] - index[:, None] + radius
    count = taps.shape[0]
    onehot = (offset[None, :, :] == jnp.arange(count, dtype=jnp.int32)[:, None, None]).astype(jnp.float32)
    return jnp.sum(onehot * taps[:, None, None], axis=0)


def along_axial(field, matrix):
    flat = field.reshape(-1, field.shape[2])
    out = jnp.dot(flat, matrix, precision=lax.Precision.HIGHEST, preferred_element_type=jnp.float32)
    return out.reshape(field.shape)


def along_second(field, taps, reverse):
    count = taps.shape[0]
    radius = (count - 1) // 2
    length = field.shape[1]
    padded = jnp.pad(field, ((0, 0), (radius, radius), (0, 0)))
    total = jnp.zeros(field.shape, jnp.float32)
    for tap in range(count):
        start = tap if reverse else 2 * radius - tap
        total = total + taps[tap] * padded[:, start:start + length, :]
    return total


def along_first(padded, taps, reverse):
    count = taps.shape[0]
    radius = (count - 1) // 2
    length = padded.shape[0] - 2 * radius
    total = jnp.zeros((length,) + padded.shape[1:], jnp.float32)
    for tap in range(count):
        start = tap if reverse else 2 * radius - tap
        total = total + taps[tap] * padded[start:start + length]
    return total


def pad_first(field, radius):
    return jnp.pad(field, ((radius, radius), (0, 0), (0, 0)))


def one_view(current, image, first, second, axial):
    radius = (first.shape[0] - 1) // 2
    matrix = toeplitz(axial, current.shape[2], (axial.shape[0] - 1) // 2)
    inner = along_second(along_axial(current, matrix), second, False)
    blurred = along_first(pad_first(inner, radius), first, False)
    ratio = image / blurred
    inner = along_second(along_axial(ratio, matrix.T), second, True)
    return along_first(pad_first(inner, radius), first, True)


def reference(estimate, images, taps_first, taps_second, taps_axial):
    current = estimate
    for step in range(ITERS):
        def accumulate(carry, items):
            return carry + one_view(current, items[0], items[1], items[2], items[3]), None

        total, unused = lax.scan(accumulate, jnp.zeros(current.shape, jnp.float32), (images, taps_first, taps_second, taps_axial))
        current = current * (total / VIEWS)
    return current
```

```python
import functools

import jax
import jax.numpy as jnp
from jax import lax
from jax.experimental import pallas as pl
from jax.experimental.pallas import tpu as pltpu
from jax.sharding import PartitionSpec as P

ITERS = 2
LANES = 128
COLS = 24


def split(x):
    high = x.astype(jnp.bfloat16)
    low = (x - high.astype(jnp.float32)).astype(jnp.bfloat16)
    return high, low


def product(x, m_high, m_low):
    x_high, x_low = split(x)
    dot = functools.partial(jnp.dot, preferred_element_type=jnp.float32)
    return dot(x_high, m_high) + (dot(x_high, m_low) + dot(x_low, m_high))


def banded(row, radius):
    full = jnp.broadcast_to(row, (LANES, LANES))
    rolled = pltpu.roll(full, LANES - radius, 1, stride=1, stride_axis=0)
    z = lax.broadcasted_iota(jnp.int32, (LANES, LANES), 0)
    zz = lax.broadcasted_iota(jnp.int32, (LANES, LANES), 1)
    return jnp.where(jnp.abs(zz - z) <= radius, rolled, 0.0)


def edges(flag, low, high):
    even = flag == 0
    return jnp.where(even, high, low), jnp.where(even, low, high)


def views_pass(sizes, flags, est_ref, data_ref, part_ref, near_ref, far_ref, shifted, spread):
    nf, ns, rz = sizes
    rows, cols, halo_x = 8, 16, nf - 1
    wide = rows + halo_x
    views = data_ref.shape[0]
    for k in range(ns):
        shifted[k] = est_ref[:, k : k + cols, :]

    def one(v, carry):
        taps = data_ref[v, rows * cols : rows * cols + 8, :]
        first = [jnp.broadcast_to(taps[2:3, i : i + 1], (cols, LANES)) for i in range(nf)]
        second = [
            jnp.broadcast_to(taps[2:3, nf + i : nf + i + 1], (cols, LANES)) for i in range(ns)
        ]
        conv = split(banded(taps[0:1], rz))
        corr = split(banded(taps[1:2], rz))
        a = []
        for i in range(wide):
            t = second[0] * shifted[ns - 1, i]
            for k in range(1, ns):
                t = t + second[k] * shifted[ns - 1 - k, i]
            a.append(t)
        b = []
        for i in range(rows):
            t = first[0] * a[i + nf - 1]
            for k in range(1, nf):
                t = t + first[k] * a[i + nf - 1 - k]
            b.append(t)
        blurred = product(jnp.concatenate(b, axis=0), *conv)
        ratio = data_ref[v, 0 : rows * cols, :] / blurred
        back = product(ratio, *corr)
        for i in range(wide):
            t = None
            for k in range(nf):
                j = i - (nf - 1) + k
                if 0 <= j < rows:
                    u = first[k] * back[j * cols : (j + 1) * cols]
                    t = u if t is None else t + u
            spread[v, i] = t
        return carry

    lax.fori_loop(0, views, one, 0)

    part_ref[...] = jnp.zeros_like(part_ref)

    def row(i, carry):
        sums = [None] * ns
        for v in range(views):
            taps = data_ref[v, rows * cols + 2 : rows * cols + 3, :]
            g = spread[v, i]
            for k in range(ns):
                u = jnp.broadcast_to(taps[:, nf + ns - 1 - k : nf + ns - k], (cols, LANES)) * g
                sums[k] = u if sums[k] is None else sums[k] + u
        for k in range(ns):
            part_ref[i, k : k + cols, :] += sums[k]
        return carry

    lax.fori_loop(0, wide, row, 0)
    near_ref[...], far_ref[...] = edges(
        flags[0], part_ref[0:halo_x], part_ref[wide - halo_x : wide]
    )


def pass_kernel(sizes, flags, est_ref, data_ref, part_ref, near_ref, far_ref, shifted, spread):
    views_pass(sizes, flags, est_ref, data_ref, part_ref, near_ref, far_ref, shifted, spread)


def update_kernel(sizes, views, flags, est_ref, total_ref, yn_ref, yf_ref, data_ref, new_ref, part_ref, near_ref, far_ref, shifted, spread):
    even = flags[1] == 0
    low = jnp.where(even, yf_ref[...], yn_ref[...])
    high = jnp.where(even, yn_ref[...], yf_ref[...])
    new_ref[:, 0:8, :] = est_ref[:, 0:8, :] * ((total_ref[:, 0:8, :] + low) / views)
    new_ref[:, 8:16, :] = est_ref[:, 8:16, :] * (total_ref[:, 8:16, :] / views)
    new_ref[:, 16:24, :] = est_ref[:, 16:24, :] * ((total_ref[:, 16:24, :] + high) / views)
    views_pass(sizes, flags, new_ref, data_ref, part_ref, near_ref, far_ref, shifted, spread)


def rows_kernel(flags, part_ref, near_ref, far_ref, out_ref, yn_ref, yf_ref):
    wide, halo = part_ref.shape[0], near_ref.shape[0]
    even = flags[0] == 0
    near, far = near_ref[...], far_ref[...]
    out_ref[0:halo] = part_ref[0:halo] + jnp.where(even, far, near)
    out_ref[halo : wide - halo] = part_ref[halo : wide - halo]
    out_ref[wide - halo : wide] = part_ref[wide - halo : wide] + jnp.where(even, near, far)
    yn_ref[...], yf_ref[...] = edges(flags[1], out_ref[:, 0:8, :], out_ref[:, 16:24, :])


def final_kernel(views, lo_x, lo_y, flags, est_ref, total_ref, yn_ref, yf_ref, out_ref, sums):
    even = flags[1] == 0
    low = jnp.where(even, yf_ref[...], yn_ref[...])
    high = jnp.where(even, yn_ref[...], yf_ref[...])
    sums[:, 0:8, :] = est_ref[:, 0:8, :] * ((total_ref[:, 0:8, :] + low) / views)
    sums[:, 8:16, :] = est_ref[:, 8:16, :] * (total_ref[:, 8:16, :] / views)
    sums[:, 16:24, :] = est_ref[:, 16:24, :] * ((total_ref[:, 16:24, :] + high) / views)
    out_ref[...] = sums[lo_x : lo_x + 8, lo_y : lo_y + 16, :]


def pairs(count, start):
    out = []
    for i in range(start, count - 1, 2):
        out += [(i, i + 1), (i + 1, i)]
    return out


def swapped(near, far, axis):
    count = lax.axis_size(axis)
    far = lax.ppermute(far, axis, pairs(count, 1))
    near = lax.ppermute(near, axis, pairs(count, 0))
    return near, far


VMEM = pl.BlockSpec(memory_space=pltpu.VMEM)
SMEM = pl.BlockSpec(memory_space=pltpu.SMEM)


def call(kernel, ins, shapes, scratch=(), cost=None):
    return pl.pallas_call(
        kernel,
        in_specs=[SMEM] + [VMEM] * (len(ins) - 1),
        out_specs=[VMEM] * len(shapes),
        out_shape=[jax.ShapeDtypeStruct(s, jnp.float32) for s in shapes],
        scratch_shapes=list(scratch),
        cost_estimate=cost,
    )(*ins)


def local(estimate, images, taps_first, taps_second, taps_axial):
    nf, ns, nz = taps_first.shape[1], taps_second.shape[1], taps_axial.shape[1]
    sizes = (nf, ns, (nz - 1) // 2)
    views = lax.axis_size("view")
    rows, cols, lanes = estimate.shape
    wide = rows + nf - 1
    halo = nf - 1
    flags = jnp.stack(
        [lax.axis_index("tile") % 2, lax.axis_index("view") % 2]
    ).astype(jnp.int32)

    own = jnp.pad(estimate, ((nf // 2, nf // 2), (ns // 2, COLS - cols - ns // 2), (0, 0)))
    near, far = edges(flags[0], own[0:halo], own[wide - halo :])
    near, far = swapped(near, far, "tile")

    pieces = images[0].reshape(rows, views, cols, lanes).transpose(1, 0, 2, 3)
    pieces = pieces.reshape(views, rows * cols, lanes)
    pad = lambda x: jnp.pad(x, ((0, 0), (0, lanes - x.shape[1])))
    taps = jnp.concatenate(
        [
            pad(taps_axial),
            pad(taps_axial[:, ::-1]),
            pad(jnp.concatenate([taps_first, taps_second], axis=1)),
            jnp.zeros((5, lanes), jnp.float32),
        ],
        axis=0,
    )
    data = jnp.concatenate([pieces, jnp.broadcast_to(taps[None], (views, 8, lanes))], axis=1)
    data = lax.all_to_all(data, "view", 0, 0, tiled=True)

    block, strip, side = (wide, COLS, lanes), (halo, COLS, lanes), (wide, 8, lanes)
    scratch = [
        pltpu.VMEM((ns, wide, cols, lanes), jnp.float32),
        pltpu.VMEM((views, wide, cols, lanes), jnp.float32),
    ]

    def joined(part, near, far):
        total, yn, yf = call(rows_kernel, (flags, part, near, far), (block, side, side))
        yn, yf = swapped(yn, yf, "view")
        return total, yn, yf

    total, yn, yf = joined(own, near, far)
    even = flags[1] == 0
    low, high = jnp.where(even, yf, yn), jnp.where(even, yn, yf)
    current = jnp.concatenate(
        [total[:, 0:8] + low, total[:, 8:16], total[:, 16:24] + high], axis=1
    )
    part, near, far = call(
        functools.partial(pass_kernel, sizes), (flags, current, data), (block, strip, strip), scratch
    )
    for step in range(1, ITERS):
        near, far = swapped(near, far, "tile")
        total, yn, yf = joined(part, near, far)
        current, part, near, far = call(
            functools.partial(update_kernel, sizes, views),
            (flags, current, total, yn, yf, data),
            (block, block, strip, strip),
            scratch,
        )
    near, far = swapped(near, far, "tile")
    total, yn, yf = joined(part, near, far)
    (out,) = call(
        functools.partial(final_kernel, views, nf // 2, ns // 2),
        (flags, current, total, yn, yf),
        ((rows, cols, lanes),),
        [pltpu.VMEM(block, jnp.float32)],
    )
    return out


def solution(mesh):
    in_specs = (
        P("tile", "view", None),
        P("view", "tile", None, None),
        P("view", None),
        P("view", None),
        P("view", None),
    )
    out_specs = P("tile", "view", None)
    return jax.shard_map(local, mesh=mesh, in_specs=in_specs, out_specs=out_specs, check_vma=False)
```

```python
import functools

import jax
import jax.numpy as jnp
from jax import lax
from jax.experimental import pallas as pl
from jax.experimental.pallas import tpu as pltpu
from jax.sharding import PartitionSpec as P

ITERS = 2
LANES = 128
COLS = 24
ROWS, WIDTH = 8, 16


def split(x):
    high = x.astype(jnp.bfloat16)
    low = (x - high.astype(jnp.float32)).astype(jnp.bfloat16)
    return high, low


def stacked(x):
    high, low = split(x)
    return jnp.concatenate([high, low, high], axis=1)


def banded(row, radius):
    full = jnp.broadcast_to(row, (LANES, LANES))
    rolled = pltpu.roll(full, LANES - radius, 1, stride=1, stride_axis=0)
    z = lax.broadcasted_iota(jnp.int32, (LANES, LANES), 0)
    zz = lax.broadcasted_iota(jnp.int32, (LANES, LANES), 1)
    return jnp.where(jnp.abs(zz - z) <= radius, rolled, 0.0)


def edges(flag, low, high):
    even = flag == 0
    return jnp.where(even, high, low), jnp.where(even, low, high)


def tables_kernel(radius, count, flags, taps_ref, conv_ref, corr_ref, table_ref):
    lane = lax.broadcasted_iota(jnp.int32, (16, LANES), 1)
    sub = lax.broadcasted_iota(jnp.int32, (16, LANES), 0)

    def one(v, carry):
        taps = taps_ref[pl.ds(8 * v, 8), :]
        for row, ref in ((0, conv_ref), (1, corr_ref)):
            high, low = split(banded(taps[row : row + 1], radius))
            ref[v, 0:LANES] = high
            ref[v, LANES : 2 * LANES] = high
            ref[v, 2 * LANES : 3 * LANES] = low
        picked = jnp.where(lane == sub, jnp.broadcast_to(taps[2:3], (16, LANES)), 0.0)
        column = jnp.broadcast_to(jnp.sum(picked, axis=1, keepdims=True), (16, LANES))
        for k in range(count):
            table_ref[v, k] = jnp.broadcast_to(column[k : k + 1], (8, LANES))
        return carry

    lax.fori_loop(0, table_ref.shape[0], one, 0)


def conv_part(sizes, est_ref, conv_ref, table_ref, spread, finish):
    nf, ns = sizes
    wide, views = est_ref.shape[0], conv_ref.shape[0]

    def row(i, carry):
        shifted = [
            [est_ref[i, k + 8 * h : k + 8 * h + 8, :] for h in range(2)] for k in range(ns)
        ]
        for v in range(views):
            taps = [table_ref[v, nf + ns - 1 - k] for k in range(ns)]
            for h in range(2):
                t = taps[0] * shifted[0][h]
                for k in range(1, ns):
                    t = t + taps[k] * shifted[k][h]
                spread[v, i, 8 * h : 8 * h + 8, :] = t
        return carry

    lax.fori_loop(0, wide, row, 0)

    def one(v, carry):
        first = [table_ref[v, k] for k in range(nf)]
        out = []
        for i in range(ROWS):
            for h in range(2):
                t = first[0] * spread[v, i + nf - 1, 8 * h : 8 * h + 8, :]
                for k in range(1, nf):
                    t = t + first[k] * spread[v, i + nf - 1 - k, 8 * h : 8 * h + 8, :]
                out.append(t)
        x = stacked(jnp.concatenate(out, axis=0))
        finish(v, jnp.dot(x, conv_ref[v], preferred_element_type=jnp.float32))
        return carry

    lax.fori_loop(0, views, one, 0, unroll=2)


def corr_part(sizes, flags, ratio_of, corr_ref, table_ref, spread, part_ref, near_ref, far_ref):
    nf, ns = sizes
    wide, views = spread.shape[1], spread.shape[0]

    def one(v, carry):
        first = [table_ref[v, k] for k in range(nf)]
        back = jnp.dot(stacked(ratio_of(v)), corr_ref[v], preferred_element_type=jnp.float32)
        for i in range(wide):
            for h in range(2):
                t = None
                for k in range(nf):
                    j = i - (nf - 1) + k
                    if 0 <= j < ROWS:
                        at = j * WIDTH + 8 * h
                        u = first[k] * back[at : at + 8]
                        t = u if t is None else t + u
                spread[v, i, 8 * h : 8 * h + 8, :] = t
        return carry

    lax.fori_loop(0, views, one, 0, unroll=2)

    def row(i, carry):
        sums = [[None, None] for _ in range(ns)]
        for v in range(views):
            g = [spread[v, i, 8 * h : 8 * h + 8, :] for h in range(2)]
            for k in range(ns):
                tap = table_ref[v, nf + ns - 1 - k]
                for h in range(2):
                    u = tap * g[h]
                    sums[k][h] = u if sums[k][h] is None else sums[k][h] + u
        total = None
        for k in range(ns):
            t = jnp.concatenate(sums[k] + [jnp.zeros((8, LANES), jnp.float32)], axis=0)
            t = pltpu.roll(t, k, 0) if k else t
            total = t if total is None else total + t
        part_ref[i] = total
        return carry

    lax.fori_loop(0, wide, row, 0)
    halo = nf - 1
    near_ref[...], far_ref[...] = edges(
        flags[0], part_ref[0:halo], part_ref[wide - halo : wide]
    )


def sides(flags, yn_ref, yf_ref):
    even = flags[1] == 0
    yn, yf = yn_ref[...], yf_ref[...]
    return jnp.where(even, yf, yn), jnp.where(even, yn, yf)


def first_conv_kernel(sizes, flags, total_ref, yn_ref, yf_ref, conv_ref, table_ref, est_ref, blurred_ref, spread):
    low, high = sides(flags, yn_ref, yf_ref)
    est_ref[:, 0:8, :] = total_ref[:, 0:8, :] + low
    est_ref[:, 8:16, :] = total_ref[:, 8:16, :]
    est_ref[:, 16:24, :] = total_ref[:, 16:24, :] + high

    def finish(v, blurred):
        blurred_ref[v] = blurred

    conv_part(sizes, est_ref, conv_ref, table_ref, spread, finish)


def first_corr_kernel(sizes, flags, data_ref, blurred_ref, corr_ref, table_ref, part_ref, near_ref, far_ref, spread):
    corr_part(
        sizes, flags, lambda v: data_ref[v] / blurred_ref[v],
        corr_ref, table_ref, spread, part_ref, near_ref, far_ref,
    )


def updated(views, flags, est_ref, total_ref, yn_ref, yf_ref, new_ref):
    low, high = sides(flags, yn_ref, yf_ref)
    new_ref[:, 0:8, :] = est_ref[:, 0:8, :] * ((total_ref[:, 0:8, :] + low) / views)
    new_ref[:, 8:16, :] = est_ref[:, 8:16, :] * (total_ref[:, 8:16, :] / views)
    new_ref[:, 16:24, :] = est_ref[:, 16:24, :] * ((total_ref[:, 16:24, :] + high) / views)


def pass_kernel(sizes, views, flags, est_ref, total_ref, yn_ref, yf_ref, data_ref, conv_ref, corr_ref, table_ref, new_ref, part_ref, near_ref, far_ref, spread, ratio):
    updated(views, flags, est_ref, total_ref, yn_ref, yf_ref, new_ref)

    def finish(v, blurred):
        ratio[v] = data_ref[v] / blurred

    conv_part(sizes, new_ref, conv_ref, table_ref, spread, finish)
    corr_part(
        sizes, flags, lambda v: ratio[v],
        corr_ref, table_ref, spread, part_ref, near_ref, far_ref,
    )


def rows_kernel(flags, part_ref, near_ref, far_ref, out_ref, yn_ref, yf_ref):
    wide, halo = part_ref.shape[0], near_ref.shape[0]
    even = flags[0] == 0
    near, far = near_ref[...], far_ref[...]
    out_ref[0:halo] = part_ref[0:halo] + jnp.where(even, far, near)
    out_ref[halo : wide - halo] = part_ref[halo : wide - halo]
    out_ref[wide - halo : wide] = part_ref[wide - halo : wide] + jnp.where(even, near, far)
    yn_ref[...], yf_ref[...] = edges(flags[1], out_ref[:, 0:8, :], out_ref[:, 16:24, :])


def final_kernel(views, lo_x, lo_y, flags, est_ref, total_ref, yn_ref, yf_ref, out_ref, new):
    updated(views, flags, est_ref, total_ref, yn_ref, yf_ref, new)
    out_ref[...] = new[lo_x : lo_x + ROWS, lo_y : lo_y + WIDTH, :]


def pairs(count, start):
    out = []
    for i in range(start, count - 1, 2):
        out += [(i, i + 1), (i + 1, i)]
    return out


def swapped(near, far, axis):
    count = lax.axis_size(axis)
    far = lax.ppermute(far, axis, pairs(count, 1))
    near = lax.ppermute(near, axis, pairs(count, 0))
    return near, far


VMEM = pl.BlockSpec(memory_space=pltpu.VMEM)
SMEM = pl.BlockSpec(memory_space=pltpu.SMEM)


def call(kernel, ins, shapes, scratch=(), limit=2 << 20):
    shapes = [s if isinstance(s, jax.ShapeDtypeStruct) else jax.ShapeDtypeStruct(s, jnp.float32) for s in shapes]
    return pl.pallas_call(
        kernel,
        in_specs=[SMEM] + [VMEM] * (len(ins) - 1),
        out_specs=[VMEM] * len(shapes),
        out_shape=shapes,
        scratch_shapes=list(scratch),
        compiler_params=pltpu.CompilerParams(vmem_limit_bytes=limit),
    )(*ins)


def local(estimate, images, taps_first, taps_second, taps_axial):
    nf, ns, nz = taps_first.shape[1], taps_second.shape[1], taps_axial.shape[1]
    sizes = (nf, ns)
    views = lax.axis_size("view")
    rows, cols, lanes = estimate.shape
    halo = nf - 1
    wide = rows + halo
    flags = jnp.stack(
        [lax.axis_index("tile") % 2, lax.axis_index("view") % 2]
    ).astype(jnp.int32)

    own = jnp.pad(estimate, ((nf // 2, nf // 2), (ns // 2, COLS - cols - ns // 2), (0, 0)))
    near, far = edges(flags[0], own[0:halo], own[wide - halo :])
    near, far = swapped(near, far, "tile")

    pieces = images[0].reshape(rows, views, cols, lanes).transpose(1, 0, 2, 3)
    pieces = pieces.reshape(views, rows * cols, lanes)
    data = lax.all_to_all(pieces, "view", 0, 0, tiled=True)

    pad = lambda x: jnp.pad(x, ((0, 0), (0, lanes - x.shape[1])))
    taps = jnp.concatenate(
        [
            pad(taps_axial),
            pad(taps_axial[:, ::-1]),
            pad(jnp.concatenate([taps_first, taps_second], axis=1)),
            jnp.zeros((5, lanes), jnp.float32),
        ],
        axis=0,
    )
    taps = lax.all_gather(taps, "view", axis=0, tiled=True)
    matrices = jax.ShapeDtypeStruct((views, 3 * lanes, lanes), jnp.bfloat16)
    conv, corr, table = call(
        functools.partial(tables_kernel, (nz - 1) // 2, nf + ns),
        (flags, taps),
        (matrices, matrices, (views, nf + ns, 8, lanes)),
        limit=8 << 20,
    )

    block, strip, side = (wide, COLS, lanes), (halo, COLS, lanes), (wide, 8, lanes)
    images_shape = (views, rows * cols, lanes)
    spread = pltpu.VMEM((views, wide, cols, lanes), jnp.float32)

    def joined(part, near, far):
        total, yn, yf = call(rows_kernel, (flags, part, near, far), (block, side, side))
        yn, yf = swapped(yn, yf, "view")
        return total, yn, yf

    total, yn, yf = joined(own, near, far)
    current, blurred = call(
        functools.partial(first_conv_kernel, sizes),
        (flags, total, yn, yf, conv, table),
        (block, images_shape),
        [spread],
        limit=8 << 20,
    )
    part, near, far = call(
        functools.partial(first_corr_kernel, sizes),
        (flags, data, blurred, corr, table),
        (block, strip, strip),
        [spread],
        limit=10 << 20,
    )
    for _ in range(1, ITERS):
        near, far = swapped(near, far, "tile")
        total, yn, yf = joined(part, near, far)
        current, part, near, far = call(
            functools.partial(pass_kernel, sizes, views),
            (flags, current, total, yn, yf, data, conv, corr, table),
            (block, block, strip, strip),
            [spread, pltpu.VMEM(images_shape, jnp.float32)],
            limit=12 << 20,
        )
    near, far = swapped(near, far, "tile")
    total, yn, yf = joined(part, near, far)
    (out,) = call(
        functools.partial(final_kernel, views, nf // 2, ns // 2),
        (flags, current, total, yn, yf),
        ((rows, cols, lanes),),
        [pltpu.VMEM(block, jnp.float32)],
    )
    return out


def solution(mesh):
    in_specs = (
        P("tile", "view", None),
        P("view", "tile", None, None),
        P("view", None),
        P("view", None),
        P("view", None),
    )
    out_specs = P("tile", "view", None)
    return jax.shard_map(local, mesh=mesh, in_specs=in_specs, out_specs=out_specs, check_vma=False)
```

```python
import functools

import jax
import jax.numpy as jnp
from jax import lax
from jax.experimental import pallas as pl
from jax.experimental.pallas import tpu as pltpu
from jax.sharding import PartitionSpec as P

ITERS = 2
LANES = 128
COLS = 24
ROWS, WIDTH = 8, 16
BLOCK = ROWS * WIDTH


def split(x):
    high = x.astype(jnp.bfloat16)
    low = (x - high.astype(jnp.float32)).astype(jnp.bfloat16)
    return high, low


def stacked(x):
    high, low = split(x)
    return jnp.concatenate([high, low, high], axis=1)


def banded(row, radius):
    full = jnp.broadcast_to(row, (LANES, LANES))
    rolled = pltpu.roll(full, LANES - radius, 1, stride=1, stride_axis=0)
    z = lax.broadcasted_iota(jnp.int32, (LANES, LANES), 0)
    zz = lax.broadcasted_iota(jnp.int32, (LANES, LANES), 1)
    return jnp.where(jnp.abs(zz - z) <= radius, rolled, 0.0)


def edges(flag, low, high):
    even = flag == 0
    return jnp.where(even, high, low), jnp.where(even, low, high)


def pieces_kernel(images_ref, first_ref, second_ref, axial_ref, out_ref, taps):
    taps[...] = jnp.zeros_like(taps)
    for row, ref in enumerate((axial_ref, first_ref, second_ref)):
        taps[row : row + 1, 0 : ref.shape[1]] = ref[...]
    for w in range(out_ref.shape[0]):
        for i in range(ROWS):
            out_ref[w, WIDTH * i : WIDTH * (i + 1), :] = images_ref[0, i, WIDTH * w : WIDTH * (w + 1), :]
        out_ref[w, BLOCK:, :] = taps[...]


def make_tables(sizes, data_ref, conv_ref, corr_ref, table_ref, axial):
    nf, ns, nz = sizes
    views = data_ref.shape[0]
    lane = lax.broadcasted_iota(jnp.int32, (8, LANES), 1)
    sub = lax.broadcasted_iota(jnp.int32, (8, LANES), 0)
    for v in range(views):
        axial[v : v + 1, :] = data_ref[v, BLOCK : BLOCK + 1, :]
    z = lax.broadcasted_iota(jnp.int32, (LANES, LANES), 0)
    zz = lax.broadcasted_iota(jnp.int32, (LANES, LANES), 1)
    reverse = jnp.where(z + zz == nz - 1, 1.0, 0.0).astype(jnp.float32)
    axial[views:, :] = jnp.dot(
        axial[0:views, :], reverse, precision=lax.Precision.HIGHEST, preferred_element_type=jnp.float32
    )

    def one(v, carry):
        for at, ref in ((0, conv_ref), (views, corr_ref)):
            high, low = split(banded(axial[pl.ds(at + v, 1), :], nz // 2))
            ref[v, 0:LANES] = high
            ref[v, LANES : 2 * LANES] = high
            ref[v, 2 * LANES : 3 * LANES] = low
        start = 0
        for row, count in ((1, nf), (2, ns)):
            taps = jnp.broadcast_to(data_ref[v, BLOCK + row : BLOCK + row + 1, :], (8, LANES))
            column = jnp.sum(jnp.where(lane == sub, taps, 0.0), axis=1, keepdims=True)
            column = jnp.broadcast_to(column, (8, LANES))
            for k in range(count):
                table_ref[v, start + k] = jnp.broadcast_to(column[k : k + 1], (8, LANES))
            start += count
        return carry

    lax.fori_loop(0, views, one, 0, unroll=2)


def conv_part(sizes, est_ref, conv_ref, table_ref, spread, finish):
    nf, ns, _ = sizes
    wide, views = est_ref.shape[0], conv_ref.shape[0]

    def row(i, carry):
        shifted = [
            [est_ref[i, k + 8 * h : k + 8 * h + 8, :] for h in range(2)] for k in range(ns)
        ]
        for v in range(views):
            taps = [table_ref[v, nf + ns - 1 - k] for k in range(ns)]
            for h in range(2):
                t = taps[0] * shifted[0][h]
                for k in range(1, ns):
                    t = t + taps[k] * shifted[k][h]
                spread[v, i, 8 * h : 8 * h + 8, :] = t
        return carry

    lax.fori_loop(0, wide, row, 0)

    def one(v, carry):
        first = [table_ref[v, k] for k in range(nf)]
        out = []
        for i in range(ROWS):
            for h in range(2):
                t = first[0] * spread[v, i + nf - 1, 8 * h : 8 * h + 8, :]
                for k in range(1, nf):
                    t = t + first[k] * spread[v, i + nf - 1 - k, 8 * h : 8 * h + 8, :]
                out.append(t)
        x = stacked(jnp.concatenate(out, axis=0))
        finish(v, jnp.dot(x, conv_ref[v], preferred_element_type=jnp.float32))
        return carry

    lax.fori_loop(0, views, one, 0, unroll=2)


def corr_part(sizes, flags, ratio_of, corr_ref, table_ref, spread, part_ref, near_ref, far_ref):
    nf, ns, _ = sizes
    wide, views = spread.shape[1], spread.shape[0]

    def one(v, carry):
        first = [table_ref[v, k] for k in range(nf)]
        back = jnp.dot(stacked(ratio_of(v)), corr_ref[v], preferred_element_type=jnp.float32)
        for i in range(wide):
            for h in range(2):
                t = None
                for k in range(nf):
                    j = i - (nf - 1) + k
                    if 0 <= j < ROWS:
                        at = j * WIDTH + 8 * h
                        u = first[k] * back[at : at + 8]
                        t = u if t is None else t + u
                spread[v, i, 8 * h : 8 * h + 8, :] = t
        return carry

    lax.fori_loop(0, views, one, 0, unroll=2)

    def row(i, carry):
        sums = [[None, None] for _ in range(ns)]
        for v in range(views):
            g = [spread[v, i, 8 * h : 8 * h + 8, :] for h in range(2)]
            for k in range(ns):
                tap = table_ref[v, nf + ns - 1 - k]
                for h in range(2):
                    u = tap * g[h]
                    sums[k][h] = u if sums[k][h] is None else sums[k][h] + u
        total = None
        for k in range(ns):
            t = jnp.concatenate(sums[k] + [jnp.zeros((8, LANES), jnp.float32)], axis=0)
            t = pltpu.roll(t, k, 0) if k else t
            total = t if total is None else total + t
        part_ref[i] = total
        return carry

    lax.fori_loop(0, wide, row, 0)
    halo = nf - 1
    near_ref[...], far_ref[...] = edges(
        flags[0], part_ref[0:halo], part_ref[wide - halo : wide]
    )


def sides(flags, yn_ref, yf_ref):
    even = flags[1] == 0
    yn, yf = yn_ref[...], yf_ref[...]
    return jnp.where(even, yf, yn), jnp.where(even, yn, yf)


def first_kernel(sizes, flags, total_ref, yn_ref, yf_ref, data_ref, est_ref, part_ref, near_ref, far_ref, conv_ref, corr_ref, table_ref, spread, ratio, axial):
    make_tables(sizes, data_ref, conv_ref, corr_ref, table_ref, axial)
    low, high = sides(flags, yn_ref, yf_ref)
    est_ref[:, 0:8, :] = total_ref[:, 0:8, :] + low
    est_ref[:, 8:16, :] = total_ref[:, 8:16, :]
    est_ref[:, 16:24, :] = total_ref[:, 16:24, :] + high
    both_parts(sizes, flags, est_ref, data_ref, conv_ref, corr_ref, table_ref, part_ref, near_ref, far_ref, spread, ratio)


def both_parts(sizes, flags, est_ref, data_ref, conv_ref, corr_ref, table_ref, part_ref, near_ref, far_ref, spread, ratio):
    def finish(v, blurred):
        ratio[v] = data_ref[v, 0:BLOCK, :] / blurred

    conv_part(sizes, est_ref, conv_ref, table_ref, spread, finish)
    corr_part(
        sizes, flags, lambda v: ratio[v],
        corr_ref, table_ref, spread, part_ref, near_ref, far_ref,
    )


def updated(views, flags, est_ref, total_ref, yn_ref, yf_ref, new_ref):
    low, high = sides(flags, yn_ref, yf_ref)
    new_ref[:, 0:8, :] = est_ref[:, 0:8, :] * ((total_ref[:, 0:8, :] + low) / views)
    new_ref[:, 8:16, :] = est_ref[:, 8:16, :] * (total_ref[:, 8:16, :] / views)
    new_ref[:, 16:24, :] = est_ref[:, 16:24, :] * ((total_ref[:, 16:24, :] + high) / views)


def pass_kernel(sizes, views, flags, est_ref, total_ref, yn_ref, yf_ref, data_ref, conv_ref, corr_ref, table_ref, new_ref, part_ref, near_ref, far_ref, spread, ratio):
    updated(views, flags, est_ref, total_ref, yn_ref, yf_ref, new_ref)
    both_parts(sizes, flags, new_ref, data_ref, conv_ref, corr_ref, table_ref, part_ref, near_ref, far_ref, spread, ratio)


def rows_kernel(flags, part_ref, near_ref, far_ref, out_ref, yn_ref, yf_ref):
    wide, halo = part_ref.shape[0], near_ref.shape[0]
    even = flags[0] == 0
    near, far = near_ref[...], far_ref[...]
    out_ref[0:halo] = part_ref[0:halo] + jnp.where(even, far, near)
    out_ref[halo : wide - halo] = part_ref[halo : wide - halo]
    out_ref[wide - halo : wide] = part_ref[wide - halo : wide] + jnp.where(even, near, far)
    yn_ref[...], yf_ref[...] = edges(flags[1], out_ref[:, 0:8, :], out_ref[:, 16:24, :])


def final_kernel(views, lo_x, lo_y, flags, est_ref, total_ref, yn_ref, yf_ref, out_ref, new):
    updated(views, flags, est_ref, total_ref, yn_ref, yf_ref, new)
    out_ref[...] = new[lo_x : lo_x + ROWS, lo_y : lo_y + WIDTH, :]


def pairs(count, start):
    out = []
    for i in range(start, count - 1, 2):
        out += [(i, i + 1), (i + 1, i)]
    return out


def swapped(near, far, axis):
    count = lax.axis_size(axis)
    far = lax.ppermute(far, axis, pairs(count, 1))
    near = lax.ppermute(near, axis, pairs(count, 0))
    return near, far


VMEM = pl.BlockSpec(memory_space=pltpu.VMEM)
SMEM = pl.BlockSpec(memory_space=pltpu.SMEM)


def call(kernel, ins, shapes, scratch=(), limit=2 << 20):
    shapes = [s if isinstance(s, jax.ShapeDtypeStruct) else jax.ShapeDtypeStruct(s, jnp.float32) for s in shapes]
    return pl.pallas_call(
        kernel,
        in_specs=[SMEM] + [VMEM] * (len(ins) - 1),
        out_specs=[VMEM] * len(shapes),
        out_shape=shapes,
        scratch_shapes=list(scratch),
        compiler_params=pltpu.CompilerParams(vmem_limit_bytes=limit),
    )(*ins)


def local(estimate, images, taps_first, taps_second, taps_axial):
    nf, ns, nz = taps_first.shape[1], taps_second.shape[1], taps_axial.shape[1]
    sizes = (nf, ns, nz)
    views = lax.axis_size("view")
    rows, cols, lanes = estimate.shape
    halo = nf - 1
    wide = rows + halo
    flags = jnp.stack(
        [lax.axis_index("tile") % 2, lax.axis_index("view") % 2]
    ).astype(jnp.int32)

    own = jnp.pad(estimate, ((nf // 2, nf // 2), (ns // 2, COLS - cols - ns // 2), (0, 0)))
    near, far = edges(flags[0], own[0:halo], own[wide - halo :])
    near, far = swapped(near, far, "tile")

    data_shape = (views, rows * cols + 8, lanes)
    data = pl.pallas_call(
        pieces_kernel,
        in_specs=[VMEM] * 4,
        out_specs=VMEM,
        out_shape=jax.ShapeDtypeStruct(data_shape, jnp.float32),
        scratch_shapes=[pltpu.VMEM((8, lanes), jnp.float32)],
        compiler_params=pltpu.CompilerParams(vmem_limit_bytes=4 << 20),
    )(images, taps_first, taps_second, taps_axial)
    data = lax.all_to_all(data, "view", 0, 0, tiled=True)
    matrices = jax.ShapeDtypeStruct((views, 3 * lanes, lanes), jnp.bfloat16)

    block, strip, side = (wide, COLS, lanes), (halo, COLS, lanes), (wide, 8, lanes)
    scratch = [
        pltpu.VMEM((views, wide, cols, lanes), jnp.float32),
        pltpu.VMEM((views, rows * cols, lanes), jnp.float32),
    ]

    def joined(part, near, far):
        total, yn, yf = call(rows_kernel, (flags, part, near, far), (block, side, side))
        yn, yf = swapped(yn, yf, "view")
        return total, yn, yf

    total, yn, yf = joined(own, near, far)
    current, part, near, far, conv, corr, table = call(
        functools.partial(first_kernel, sizes),
        (flags, total, yn, yf, data),
        (block, block, strip, strip, matrices, matrices, (views, nf + ns, 8, lanes)),
        scratch + [pltpu.VMEM((2 * views, lanes), jnp.float32)],
        limit=16 << 20,
    )
    for _ in range(1, ITERS):
        near, far = swapped(near, far, "tile")
        total, yn, yf = joined(part, near, far)
        current, part, near, far = call(
            functools.partial(pass_kernel, sizes, views),
            (flags, current, total, yn, yf, data, conv, corr, table),
            (block, block, strip, strip),
            scratch,
            limit=12 << 20,
        )
    near, far = swapped(near, far, "tile")
    total, yn, yf = joined(part, near, far)
    (out,) = call(
        functools.partial(final_kernel, views, nf // 2, ns // 2),
        (flags, current, total, yn, yf),
        ((rows, cols, lanes),),
        [pltpu.VMEM(block, jnp.float32)],
    )
    return out


def solution(mesh):
    in_specs = (
        P("tile", "view", None),
        P("view", "tile", None, None),
        P("view", None),
        P("view", None),
        P("view", None),
    )
    out_specs = P("tile", "view", None)
    return jax.shard_map(local, mesh=mesh, in_specs=in_specs, out_specs=out_specs, check_vma=False)
```

```python
import functools

import jax
import jax.numpy as jnp
from jax import lax
from jax.experimental import pallas as pl
from jax.experimental.pallas import tpu as pltpu
from jax.sharding import PartitionSpec as P

ITERS = 2
LANES = 128
COLS = 24
ROWS, WIDTH = 8, 16
BLOCK = ROWS * WIDTH


def split(x):
    high = x.astype(jnp.bfloat16)
    low = (x - high.astype(jnp.float32)).astype(jnp.bfloat16)
    return high, low


def product(x, matrix):
    left = jnp.concatenate(split(x), axis=1)
    right = jnp.concatenate([matrix, matrix], axis=0)
    both = jnp.dot(left, right, preferred_element_type=jnp.float32)
    return both[:, 0:LANES] + both[:, LANES:]


def banded(row, radius):
    full = jnp.broadcast_to(row, (LANES, LANES))
    rolled = pltpu.roll(full, LANES - radius, 1, stride=1, stride_axis=0)
    z = lax.broadcasted_iota(jnp.int32, (LANES, LANES), 0)
    zz = lax.broadcasted_iota(jnp.int32, (LANES, LANES), 1)
    return jnp.where(jnp.abs(zz - z) <= radius, rolled, 0.0)


def edges(flag, low, high):
    even = flag == 0
    return jnp.where(even, high, low), jnp.where(even, low, high)


def pieces_kernel(images_ref, axial_ref, first_ref, second_ref, out_ref, rows, taps, axial, taps_1, taps_2, taps_sems, in_sems, out_sems):
    small = [
        pltpu.make_async_copy(src, dst, taps_sems.at[k])
        for k, (src, dst) in enumerate(
            ((axial_ref, axial), (first_ref, taps_1), (second_ref, taps_2))
        )
    ]
    ins = [
        pltpu.make_async_copy(images_ref.at[i], rows.at[i], in_sems.at[i]) for i in range(ROWS)
    ]
    outs = [
        pltpu.make_async_copy(
            rows.at[i], out_ref.at[:, pl.ds(WIDTH * i, WIDTH), :], out_sems.at[i]
        )
        for i in range(ROWS)
    ]
    outs.append(pltpu.make_async_copy(taps, out_ref.at[:, pl.ds(BLOCK, 8), :], out_sems.at[ROWS]))
    for copy in small + ins:
        copy.start()
    taps[...] = jnp.zeros_like(taps)
    for copy in small:
        copy.wait()
    for row, ref in enumerate((axial, taps_1, taps_2)):
        taps[:, row : row + 1, 0 : ref.shape[1]] = jnp.broadcast_to(
            ref[...][None], (taps.shape[0], 1, ref.shape[1])
        )
    outs[ROWS].start()
    for i in range(ROWS):
        ins[i].wait()
        outs[i].start()
    for copy in outs:
        copy.wait()


def make_tables(sizes, data_ref, conv_ref, corr_ref, table_ref, axial):
    _, _, nz = sizes
    views = data_ref.shape[0]
    lane = lax.broadcasted_iota(jnp.int32, (8, LANES), 1)
    sub = lax.broadcasted_iota(jnp.int32, (8, LANES), 0)
    for v in range(views):
        axial[v : v + 1, :] = data_ref[v, BLOCK : BLOCK + 1, :]
    z = lax.broadcasted_iota(jnp.int32, (LANES, LANES), 0)
    zz = lax.broadcasted_iota(jnp.int32, (LANES, LANES), 1)
    reverse = jnp.where(z + zz == nz - 1, 1.0, 0.0).astype(jnp.float32)
    axial[views:, :] = jnp.dot(
        axial[0:views, :], reverse, precision=lax.Precision.HIGHEST, preferred_element_type=jnp.float32
    )

    def one(v, carry):
        for at, ref in ((0, conv_ref), (views, corr_ref)):
            high, low = split(banded(axial[pl.ds(at + v, 1), :], nz // 2))
            ref[v, :, 0:LANES] = high
            ref[v, :, LANES:] = low
        start = 0
        for row in (1, 2):
            taps = jnp.broadcast_to(data_ref[v, BLOCK + row : BLOCK + row + 1, :], (8, LANES))
            column = jnp.sum(jnp.where(lane == sub, taps, 0.0), axis=1, keepdims=True)
            table_ref[v, start : start + 8, :] = jnp.broadcast_to(column, (8, LANES))
            start += 8
        return carry

    lax.fori_loop(0, views, one, 0, unroll=2)


def tap(table_ref, v, k):
    return jnp.broadcast_to(table_ref[v, pl.ds(k, 1), :], (8, LANES))


def conv_part(sizes, est_ref, conv_ref, table_ref, spread, finish):
    nf, ns, _ = sizes
    wide, views = est_ref.shape[0], conv_ref.shape[0]

    def row(i, carry):
        shifted = [
            [est_ref[i, k + 8 * h : k + 8 * h + 8, :] for h in range(2)] for k in range(ns)
        ]
        for v in range(views):
            taps = [tap(table_ref, v, 8 + ns - 1 - k) for k in range(ns)]
            for h in range(2):
                t = taps[0] * shifted[0][h]
                for k in range(1, ns):
                    t = t + taps[k] * shifted[k][h]
                spread[v, i, 8 * h : 8 * h + 8, :] = t
        return carry

    lax.fori_loop(0, wide, row, 0)

    def one(v, carry):
        first = [tap(table_ref, v, k) for k in range(nf)]
        out = []
        for i in range(ROWS):
            for h in range(2):
                t = first[0] * spread[v, i + nf - 1, 8 * h : 8 * h + 8, :]
                for k in range(1, nf):
                    t = t + first[k] * spread[v, i + nf - 1 - k, 8 * h : 8 * h + 8, :]
                out.append(t)
        finish(v, product(jnp.concatenate(out, axis=0), conv_ref[v]))
        return carry

    lax.fori_loop(0, views, one, 0, unroll=2)


def corr_part(sizes, flags, ratio_of, corr_ref, table_ref, spread, part_ref, near_ref, far_ref):
    nf, ns, _ = sizes
    wide, views = spread.shape[1], spread.shape[0]

    def one(v, carry):
        first = [tap(table_ref, v, k) for k in range(nf)]
        back = product(ratio_of(v), corr_ref[v])
        for i in range(wide):
            for h in range(2):
                t = None
                for k in range(nf):
                    j = i - (nf - 1) + k
                    if 0 <= j < ROWS:
                        at = j * WIDTH + 8 * h
                        u = first[k] * back[at : at + 8]
                        t = u if t is None else t + u
                spread[v, i, 8 * h : 8 * h + 8, :] = t
        return carry

    lax.fori_loop(0, views, one, 0, unroll=4)

    def row(i, carry):
        sums = [[None, None] for _ in range(ns)]
        for v in range(views):
            g = [spread[v, i, 8 * h : 8 * h + 8, :] for h in range(2)]
            for k in range(ns):
                t = tap(table_ref, v, 8 + ns - 1 - k)
                for h in range(2):
                    u = t * g[h]
                    sums[k][h] = u if sums[k][h] is None else sums[k][h] + u
        total = None
        for k in range(ns):
            t = jnp.concatenate(sums[k] + [jnp.zeros((8, LANES), jnp.float32)], axis=0)
            t = pltpu.roll(t, k, 0) if k else t
            total = t if total is None else total + t
        part_ref[i] = total
        return carry

    lax.fori_loop(0, wide, row, 0)
    halo = nf - 1
    near_ref[...], far_ref[...] = edges(
        flags[0], part_ref[0:halo], part_ref[wide - halo : wide]
    )


def sides(flags, yn_ref, yf_ref):
    even = flags[1] == 0
    yn, yf = yn_ref[...], yf_ref[...]
    return jnp.where(even, yf, yn), jnp.where(even, yn, yf)


def both_parts(sizes, flags, est_ref, data_ref, conv_ref, corr_ref, table_ref, part_ref, near_ref, far_ref, spread, ratio):
    def finish(v, blurred):
        ratio[v] = data_ref[v, 0:BLOCK, :] / blurred

    conv_part(sizes, est_ref, conv_ref, table_ref, spread, finish)
    corr_part(
        sizes, flags, lambda v: ratio[v],
        corr_ref, table_ref, spread, part_ref, near_ref, far_ref,
    )


def first_kernel(sizes, flags, total_ref, yn_ref, yf_ref, data_ref, est_ref, part_ref, near_ref, far_ref, conv_ref, corr_ref, table_ref, spread, ratio, axial):
    make_tables(sizes, data_ref, conv_ref, corr_ref, table_ref, axial)
    low, high = sides(flags, yn_ref, yf_ref)
    est_ref[:, 0:8, :] = total_ref[:, 0:8, :] + low
    est_ref[:, 8:16, :] = total_ref[:, 8:16, :]
    est_ref[:, 16:24, :] = total_ref[:, 16:24, :] + high
    both_parts(sizes, flags, est_ref, data_ref, conv_ref, corr_ref, table_ref, part_ref, near_ref, far_ref, spread, ratio)


def updated(views, flags, est_ref, total_ref, yn_ref, yf_ref, new_ref):
    low, high = sides(flags, yn_ref, yf_ref)
    new_ref[:, 0:8, :] = est_ref[:, 0:8, :] * ((total_ref[:, 0:8, :] + low) / views)
    new_ref[:, 8:16, :] = est_ref[:, 8:16, :] * (total_ref[:, 8:16, :] / views)
    new_ref[:, 16:24, :] = est_ref[:, 16:24, :] * ((total_ref[:, 16:24, :] + high) / views)


def pass_kernel(sizes, views, flags, est_ref, total_ref, yn_ref, yf_ref, data_ref, conv_ref, corr_ref, table_ref, new_ref, part_ref, near_ref, far_ref, spread, ratio):
    updated(views, flags, est_ref, total_ref, yn_ref, yf_ref, new_ref)
    both_parts(sizes, flags, new_ref, data_ref, conv_ref, corr_ref, table_ref, part_ref, near_ref, far_ref, spread, ratio)


def rows_kernel(flags, part_ref, near_ref, far_ref, out_ref, yn_ref, yf_ref):
    wide, halo = part_ref.shape[0], near_ref.shape[0]
    even = flags[0] == 0
    near, far = near_ref[...], far_ref[...]
    out_ref[0:halo] = part_ref[0:halo] + jnp.where(even, far, near)
    out_ref[halo : wide - halo] = part_ref[halo : wide - halo]
    out_ref[wide - halo : wide] = part_ref[wide - halo : wide] + jnp.where(even, near, far)
    yn_ref[...], yf_ref[...] = edges(flags[1], out_ref[:, 0:8, :], out_ref[:, 16:24, :])


def final_kernel(views, lo_x, lo_y, flags, est_ref, total_ref, yn_ref, yf_ref, out_ref, new):
    updated(views, flags, est_ref, total_ref, yn_ref, yf_ref, new)
    out_ref[...] = new[lo_x : lo_x + ROWS, lo_y : lo_y + WIDTH, :]


def pairs(count, start):
    out = []
    for i in range(start, count - 1, 2):
        out += [(i, i + 1), (i + 1, i)]
    return out


def swapped(near, far, axis):
    count = lax.axis_size(axis)
    far = lax.ppermute(far, axis, pairs(count, 1))
    near = lax.ppermute(near, axis, pairs(count, 0))
    return near, far


VMEM = pl.BlockSpec(memory_space=pltpu.VMEM)
SMEM = pl.BlockSpec(memory_space=pltpu.SMEM)


def call(kernel, ins, shapes, scratch=(), limit=2 << 20):
    shapes = [s if isinstance(s, jax.ShapeDtypeStruct) else jax.ShapeDtypeStruct(s, jnp.float32) for s in shapes]
    return pl.pallas_call(
        kernel,
        in_specs=[SMEM] + [VMEM] * (len(ins) - 1),
        out_specs=[VMEM] * len(shapes),
        out_shape=shapes,
        scratch_shapes=list(scratch),
        compiler_params=pltpu.CompilerParams(vmem_limit_bytes=limit),
    )(*ins)


def local(estimate, images, taps_first, taps_second, taps_axial):
    nf, ns, nz = taps_first.shape[1], taps_second.shape[1], taps_axial.shape[1]
    sizes = (nf, ns, nz)
    views = lax.axis_size("view")
    rows, cols, lanes = estimate.shape
    halo = nf - 1
    wide = rows + halo
    flags = jnp.stack(
        [lax.axis_index("tile") % 2, lax.axis_index("view") % 2]
    ).astype(jnp.int32)

    own = jnp.pad(estimate, ((nf // 2, nf // 2), (ns // 2, COLS - cols - ns // 2), (0, 0)))
    near, far = edges(flags[0], own[0:halo], own[wide - halo :])
    near, far = swapped(near, far, "tile")

    hbm = pl.BlockSpec(memory_space=pltpu.HBM)
    small = (taps_axial, taps_first, taps_second)
    data = pl.pallas_call(
        pieces_kernel,
        in_specs=[hbm] * 4,
        out_specs=hbm,
        out_shape=jax.ShapeDtypeStruct((views, rows * cols + 8, lanes), jnp.float32),
        scratch_shapes=[
            pltpu.VMEM((rows, views, cols, lanes), jnp.float32),
            pltpu.VMEM((views, 8, lanes), jnp.float32),
            *(pltpu.VMEM(x.shape, jnp.float32) for x in small),
            pltpu.SemaphoreType.DMA((3,)),
            pltpu.SemaphoreType.DMA((rows,)),
            pltpu.SemaphoreType.DMA((rows + 1,)),
        ],
        compiler_params=pltpu.CompilerParams(vmem_limit_bytes=60 << 20),
    )(images.reshape(rows, views, cols, lanes), *small)
    data = lax.all_to_all(data, "view", 0, 0, tiled=True)
    matrices = jax.ShapeDtypeStruct((views, lanes, 2 * lanes), jnp.bfloat16)

    block, strip, side = (wide, COLS, lanes), (halo, COLS, lanes), (wide, 8, lanes)
    scratch = [
        pltpu.VMEM((views, wide, cols, lanes), jnp.float32),
        pltpu.VMEM((views, rows * cols, lanes), jnp.float32),
    ]

    def joined(part, near, far):
        total, yn, yf = call(rows_kernel, (flags, part, near, far), (block, side, side))
        yn, yf = swapped(yn, yf, "view")
        return total, yn, yf

    total, yn, yf = joined(own, near, far)
    current, part, near, far, conv, corr, table = call(
        functools.partial(first_kernel, sizes),
        (flags, total, yn, yf, data),
        (block, block, strip, strip, matrices, matrices, (views, 16, lanes)),
        scratch + [pltpu.VMEM((2 * views, lanes), jnp.float32)],
        limit=16 << 20,
    )
    for _ in range(1, ITERS):
        near, far = swapped(near, far, "tile")
        total, yn, yf = joined(part, near, far)
        current, part, near, far = call(
            functools.partial(pass_kernel, sizes, views),
            (flags, current, total, yn, yf, data, conv, corr, table),
            (block, block, strip, strip),
            scratch,
            limit=12 << 20,
        )
    near, far = swapped(near, far, "tile")
    total, yn, yf = joined(part, near, far)
    (out,) = call(
        functools.partial(final_kernel, views, nf // 2, ns // 2),
        (flags, current, total, yn, yf),
        ((rows, cols, lanes),),
        [pltpu.VMEM(block, jnp.float32)],
    )
    return out


def solution(mesh):
    in_specs = (
        P("tile", "view", None),
        P("view", "tile", None, None),
        P("view", None),
        P("view", None),
        P("view", None),
    )
    out_specs = P("tile", "view", None)
    return jax.shard_map(local, mesh=mesh, in_specs=in_specs, out_specs=out_specs, check_vma=False)
```

```python
import functools

import jax
import jax.numpy as jnp
from jax import lax
from jax.experimental import pallas as pl
from jax.experimental.pallas import tpu as pltpu
from jax.sharding import PartitionSpec as P

ITERS = 2
LANES = 128
COLS = 24
ROWS, WIDTH = 8, 16
BLOCK = ROWS * WIDTH


def split(x):
    high = x.astype(jnp.bfloat16)
    low = (x - high.astype(jnp.float32)).astype(jnp.bfloat16)
    return high, low


def product(x, matrix):
    left = jnp.concatenate(split(x), axis=1)
    right = jnp.concatenate([matrix, matrix], axis=0)
    both = jnp.dot(left, right, preferred_element_type=jnp.float32)
    return both[:, 0:LANES] + both[:, LANES:]


def banded(row, radius, ref):
    full = jnp.broadcast_to(row, (16, LANES))
    first = pltpu.roll(full, LANES - radius, 1, stride=1, stride_axis=0)
    z = lax.broadcasted_iota(jnp.int32, (16, LANES), 0)
    zz = lax.broadcasted_iota(jnp.int32, (16, LANES), 1)
    for j in range(LANES // 16):
        rows = pltpu.roll(first, 16 * j, 1) if j else first
        if j in (0, LANES // 16 - 1):
            rows = jnp.where(jnp.abs(zz - z - 16 * j) <= radius, rows, 0.0)
        high, low = split(rows)
        ref[16 * j : 16 * j + 16, 0:LANES] = high
        ref[16 * j : 16 * j + 16, LANES:] = low


def edges(flag, low, high):
    even = flag == 0
    return jnp.where(even, high, low), jnp.where(even, low, high)


def pieces_kernel(images_ref, axial_ref, first_ref, second_ref, out_ref, rows, taps, axial, taps_1, taps_2, taps_sems, in_sems, out_sems):
    small = [
        pltpu.make_async_copy(src, dst, taps_sems.at[k])
        for k, (src, dst) in enumerate(
            ((axial_ref, axial), (first_ref, taps_1), (second_ref, taps_2))
        )
    ]
    ins = [
        pltpu.make_async_copy(images_ref.at[i], rows.at[i], in_sems.at[i]) for i in range(ROWS)
    ]
    outs = [
        pltpu.make_async_copy(
            rows.at[i], out_ref.at[:, pl.ds(WIDTH * i, WIDTH), :], out_sems.at[i]
        )
        for i in range(ROWS)
    ]
    outs.append(pltpu.make_async_copy(taps, out_ref.at[:, pl.ds(BLOCK, 8), :], out_sems.at[ROWS]))
    for copy in small + ins:
        copy.start()
    taps[...] = jnp.zeros_like(taps)
    for copy in small:
        copy.wait()
    for row, ref in enumerate((axial, taps_1, taps_2)):
        taps[:, row : row + 1, 0 : ref.shape[1]] = jnp.broadcast_to(
            ref[...][None], (taps.shape[0], 1, ref.shape[1])
        )
    outs[ROWS].start()
    for i in range(ROWS):
        ins[i].wait()
        outs[i].start()
    for copy in outs:
        copy.wait()


def make_tables(sizes, data_ref, conv_ref, corr_ref, table_ref, axial):
    _, _, nz = sizes
    views = data_ref.shape[0]
    lane = lax.broadcasted_iota(jnp.int32, (8, LANES), 1)
    sub = lax.broadcasted_iota(jnp.int32, (8, LANES), 0)
    for v in range(views):
        axial[v : v + 1, :] = data_ref[v, BLOCK : BLOCK + 1, :]
    z = lax.broadcasted_iota(jnp.int32, (LANES, LANES), 0)
    zz = lax.broadcasted_iota(jnp.int32, (LANES, LANES), 1)
    reverse = jnp.where(z + zz == nz - 1, 1.0, 0.0).astype(jnp.float32)
    axial[views:, :] = jnp.dot(
        axial[0:views, :], reverse, precision=lax.Precision.HIGHEST, preferred_element_type=jnp.float32
    )

    def one(v, carry):
        for at, ref in ((0, conv_ref), (views, corr_ref)):
            banded(axial[pl.ds(at + v, 1), :], nz // 2, ref.at[v])
        start = 0
        for row in (1, 2):
            taps = jnp.broadcast_to(data_ref[v, BLOCK + row : BLOCK + row + 1, :], (8, LANES))
            column = jnp.sum(jnp.where(lane == sub, taps, 0.0), axis=1, keepdims=True)
            table_ref[v, start : start + 8, :] = jnp.broadcast_to(column, (8, LANES))
            start += 8
        return carry

    lax.fori_loop(0, views, one, 0, unroll=2)


def tap(table_ref, v, k):
    return jnp.broadcast_to(table_ref[v, pl.ds(k, 1), :], (8, LANES))


def conv_part(sizes, est_ref, conv_ref, table_ref, spread, finish):
    nf, ns, _ = sizes
    wide, views = est_ref.shape[0], conv_ref.shape[0]

    def row(i, carry):
        shifted = [
            [est_ref[i, k + 8 * h : k + 8 * h + 8, :] for h in range(2)] for k in range(ns)
        ]
        for v in range(views):
            taps = [tap(table_ref, v, 8 + ns - 1 - k) for k in range(ns)]
            for h in range(2):
                t = taps[0] * shifted[0][h]
                for k in range(1, ns):
                    t = t + taps[k] * shifted[k][h]
                spread[v, i, 8 * h : 8 * h + 8, :] = t
        return carry

    lax.fori_loop(0, wide, row, 0)

    def one(v, carry):
        first = [tap(table_ref, v, k) for k in range(nf)]
        out = []
        for i in range(ROWS):
            for h in range(2):
                t = first[0] * spread[v, i + nf - 1, 8 * h : 8 * h + 8, :]
                for k in range(1, nf):
                    t = t + first[k] * spread[v, i + nf - 1 - k, 8 * h : 8 * h + 8, :]
                out.append(t)
        finish(v, product(jnp.concatenate(out, axis=0), conv_ref[v]))
        return carry

    lax.fori_loop(0, views, one, 0, unroll=2)


def corr_part(sizes, flags, ratio_of, corr_ref, table_ref, spread, part_ref, near_ref, far_ref):
    nf, ns, _ = sizes
    wide, views = spread.shape[1], spread.shape[0]

    def one(v, carry):
        first = [tap(table_ref, v, k) for k in range(nf)]
        back = product(ratio_of(v), corr_ref[v])
        for i in range(wide):
            for h in range(2):
                t = None
                for k in range(nf):
                    j = i - (nf - 1) + k
                    if 0 <= j < ROWS:
                        at = j * WIDTH + 8 * h
                        u = first[k] * back[at : at + 8]
                        t = u if t is None else t + u
                spread[v, i, 8 * h : 8 * h + 8, :] = t
        return carry

    lax.fori_loop(0, views, one, 0, unroll=4)

    def row(i, carry):
        sums = [[None, None] for _ in range(ns)]
        for v in range(views):
            g = [spread[v, i, 8 * h : 8 * h + 8, :] for h in range(2)]
            for k in range(ns):
                t = tap(table_ref, v, 8 + ns - 1 - k)
                for h in range(2):
                    u = t * g[h]
                    sums[k][h] = u if sums[k][h] is None else sums[k][h] + u
        total = None
        for k in range(ns):
            t = jnp.concatenate(sums[k] + [jnp.zeros((8, LANES), jnp.float32)], axis=0)
            t = pltpu.roll(t, k, 0) if k else t
            total = t if total is None else total + t
        part_ref[i] = total
        return carry

    lax.fori_loop(0, wide, row, 0)
    strip = near_ref.shape[0]
    near_ref[...], far_ref[...] = edges(
        flags[0], part_ref[0:strip], part_ref[wide - strip : wide]
    )


def sides(flags, yn_ref, yf_ref):
    even = flags[1] == 0
    yn, yf = yn_ref[...], yf_ref[...]
    return jnp.where(even, yf, yn), jnp.where(even, yn, yf)


def both_parts(sizes, flags, est_ref, data_ref, conv_ref, corr_ref, table_ref, part_ref, near_ref, far_ref, spread, ratio):
    def finish(v, blurred):
        ratio[v] = data_ref[v, 0:BLOCK, :] / blurred

    conv_part(sizes, est_ref, conv_ref, table_ref, spread, finish)
    corr_part(
        sizes, flags, lambda v: ratio[v],
        corr_ref, table_ref, spread, part_ref, near_ref, far_ref,
    )


def first_kernel(sizes, flags, total_ref, yn_ref, yf_ref, data_ref, est_ref, part_ref, near_ref, far_ref, conv_ref, corr_ref, table_ref, spread, ratio, axial):
    make_tables(sizes, data_ref, conv_ref, corr_ref, table_ref, axial)
    low, high = sides(flags, yn_ref, yf_ref)
    est_ref[:, 0:8, :] = total_ref[:, 0:8, :] + low
    est_ref[:, 8:16, :] = total_ref[:, 8:16, :]
    est_ref[:, 16:24, :] = total_ref[:, 16:24, :] + high
    both_parts(sizes, flags, est_ref, data_ref, conv_ref, corr_ref, table_ref, part_ref, near_ref, far_ref, spread, ratio)


def updated(views, flags, est_ref, total_ref, yn_ref, yf_ref, new_ref):
    low, high = sides(flags, yn_ref, yf_ref)
    new_ref[:, 0:8, :] = est_ref[:, 0:8, :] * ((total_ref[:, 0:8, :] + low) / views)
    new_ref[:, 8:16, :] = est_ref[:, 8:16, :] * (total_ref[:, 8:16, :] / views)
    new_ref[:, 16:24, :] = est_ref[:, 16:24, :] * ((total_ref[:, 16:24, :] + high) / views)


def pass_kernel(sizes, views, flags, est_ref, total_ref, yn_ref, yf_ref, data_ref, conv_ref, corr_ref, table_ref, new_ref, part_ref, near_ref, far_ref, spread, ratio):
    updated(views, flags, est_ref, total_ref, yn_ref, yf_ref, new_ref)
    both_parts(sizes, flags, new_ref, data_ref, conv_ref, corr_ref, table_ref, part_ref, near_ref, far_ref, spread, ratio)


def rows_kernel(flags, part_ref, near_ref, far_ref, out_ref, yn_ref, yf_ref):
    strip, rows = near_ref.shape[0], out_ref.shape[0]
    skip = (part_ref.shape[0] - rows) // 2
    even = flags[0] == 0
    near, far = near_ref[...], far_ref[...]
    out_ref[0:strip] = part_ref[skip : skip + strip] + jnp.where(even, far, near)
    out_ref[strip : rows - strip] = part_ref[skip + strip : skip + rows - strip]
    out_ref[rows - strip :] = part_ref[skip + rows - strip : skip + rows] + jnp.where(even, near, far)
    yn_ref[...], yf_ref[...] = edges(flags[1], out_ref[:, 0:8, :], out_ref[:, 16:24, :])


def final_kernel(views, lo_x, lo_y, flags, est_ref, total_ref, yn_ref, yf_ref, out_ref, total):
    low, high = sides(flags, yn_ref, yf_ref)
    total[:, 0:8, :] = total_ref[:, 0:8, :] + low
    total[:, 8:16, :] = total_ref[:, 8:16, :]
    total[:, 16:24, :] = total_ref[:, 16:24, :] + high
    own = pl.ds(lo_y, WIDTH)
    out_ref[...] = est_ref[pl.ds(lo_x, ROWS), own, :] * (total[:, own, :] / views)


def pairs(count, start):
    out = []
    for i in range(start, count - 1, 2):
        out += [(i, i + 1), (i + 1, i)]
    return out


def swapped(near, far, axis):
    count = lax.axis_size(axis)
    far = lax.ppermute(far, axis, pairs(count, 1))
    near = lax.ppermute(near, axis, pairs(count, 0))
    return near, far


VMEM = pl.BlockSpec(memory_space=pltpu.VMEM)
SMEM = pl.BlockSpec(memory_space=pltpu.SMEM)


def call(kernel, ins, shapes, scratch=(), limit=2 << 20):
    shapes = [s if isinstance(s, jax.ShapeDtypeStruct) else jax.ShapeDtypeStruct(s, jnp.float32) for s in shapes]
    return pl.pallas_call(
        kernel,
        in_specs=[SMEM] + [VMEM] * (len(ins) - 1),
        out_specs=[VMEM] * len(shapes),
        out_shape=shapes,
        scratch_shapes=list(scratch),
        compiler_params=pltpu.CompilerParams(vmem_limit_bytes=limit),
    )(*ins)


def local(estimate, images, taps_first, taps_second, taps_axial):
    nf, ns, nz = taps_first.shape[1], taps_second.shape[1], taps_axial.shape[1]
    sizes = (nf, ns, nz)
    views = lax.axis_size("view")
    rows, cols, lanes = estimate.shape
    halo = nf - 1
    wide = rows + halo
    flags = jnp.stack(
        [lax.axis_index("tile") % 2, lax.axis_index("view") % 2]
    ).astype(jnp.int32)

    own = jnp.pad(estimate, ((nf // 2, nf // 2), (ns // 2, COLS - cols - ns // 2), (0, 0)))
    near, far = edges(flags[0], own[0:halo], own[wide - halo :])
    near, far = swapped(near, far, "tile")

    hbm = pl.BlockSpec(memory_space=pltpu.HBM)
    small = (taps_axial, taps_first, taps_second)
    data = pl.pallas_call(
        pieces_kernel,
        in_specs=[hbm] * 4,
        out_specs=hbm,
        out_shape=jax.ShapeDtypeStruct((views, rows * cols + 8, lanes), jnp.float32),
        scratch_shapes=[
            pltpu.VMEM((rows, views, cols, lanes), jnp.float32),
            pltpu.VMEM((views, 8, lanes), jnp.float32),
            *(pltpu.VMEM(x.shape, jnp.float32) for x in small),
            pltpu.SemaphoreType.DMA((3,)),
            pltpu.SemaphoreType.DMA((rows,)),
            pltpu.SemaphoreType.DMA((rows + 1,)),
        ],
        compiler_params=pltpu.CompilerParams(vmem_limit_bytes=60 << 20),
    )(images.reshape(rows, views, cols, lanes), *small)
    data = lax.all_to_all(data, "view", 0, 0, tiled=True)
    matrices = jax.ShapeDtypeStruct((views, lanes, 2 * lanes), jnp.bfloat16)

    block = (wide, COLS, lanes)
    strips = [(halo, COLS, lanes)] * (ITERS - 1) + [(halo // 2, COLS, lanes)]
    scratch = [
        pltpu.VMEM((views, wide, cols, lanes), jnp.float32),
        pltpu.VMEM((views, rows * cols, lanes), jnp.float32),
    ]

    def joined(part, near, far, count):
        shapes = [(count, width, lanes) for width in (COLS, 8, 8)]
        total, yn, yf = call(rows_kernel, (flags, part, near, far), shapes)
        yn, yf = swapped(yn, yf, "view")
        return total, yn, yf

    total, yn, yf = joined(own, near, far, wide)
    current, part, near, far, conv, corr, table = call(
        functools.partial(first_kernel, sizes),
        (flags, total, yn, yf, data),
        (block, block, strips[0], strips[0], matrices, matrices, (views, 16, lanes)),
        scratch + [pltpu.VMEM((2 * views, lanes), jnp.float32)],
        limit=16 << 20,
    )
    for step in range(1, ITERS):
        near, far = swapped(near, far, "tile")
        total, yn, yf = joined(part, near, far, wide)
        current, part, near, far = call(
            functools.partial(pass_kernel, sizes, views),
            (flags, current, total, yn, yf, data, conv, corr, table),
            (block, block, strips[step], strips[step]),
            scratch,
            limit=12 << 20,
        )
    near, far = swapped(near, far, "tile")
    total, yn, yf = joined(part, near, far, rows)
    (out,) = call(
        functools.partial(final_kernel, views, nf // 2, ns // 2),
        (flags, current, total, yn, yf),
        ((rows, cols, lanes),),
        [pltpu.VMEM((rows, COLS, lanes), jnp.float32)],
    )
    return out


def solution(mesh):
    in_specs = (
        P("tile", "view", None),
        P("view", "tile", None, None),
        P("view", None),
        P("view", None),
        P("view", None),
    )
    out_specs = P("tile", "view", None)
    return jax.shard_map(local, mesh=mesh, in_specs=in_specs, out_specs=out_specs, check_vma=False)
```

```python
import functools

import jax
import jax.numpy as jnp
from jax import lax
from jax.experimental import pallas as pl
from jax.experimental.pallas import tpu as pltpu
from jax.sharding import PartitionSpec as P

ITERS = 2
LANES = 128
COLS = 24
ROWS, WIDTH = 8, 16
BLOCK = ROWS * WIDTH


def split(x):
    high = x.astype(jnp.bfloat16)
    low = (x - high.astype(jnp.float32)).astype(jnp.bfloat16)
    return high, low


def product(x, matrix):
    left = jnp.concatenate(split(x), axis=1)
    right = jnp.concatenate([matrix, matrix], axis=0)
    both = jnp.dot(left, right, preferred_element_type=jnp.float32)
    return both[:, 0:LANES] + both[:, LANES:]


def product_t(x, matrix):
    left = jnp.concatenate(split(x), axis=1)
    high, low = matrix[:, 0:LANES], matrix[:, LANES:]
    right = jnp.concatenate(
        [jnp.concatenate([high, high], axis=1), jnp.concatenate([low, low], axis=1)], axis=0
    )
    both = lax.dot_general(
        left, right, (((1,), (1,)), ((), ())), preferred_element_type=jnp.float32
    )
    return both[:, 0:LANES] + both[:, LANES:]


def banded(row, radius, ref):
    full = jnp.broadcast_to(row, (16, LANES))
    first = pltpu.roll(full, LANES - radius, 1, stride=1, stride_axis=0)
    z = lax.broadcasted_iota(jnp.int32, (16, LANES), 0)
    zz = lax.broadcasted_iota(jnp.int32, (16, LANES), 1)
    for j in range(LANES // 16):
        rows = pltpu.roll(first, 16 * j, 1) if j else first
        if j in (0, LANES // 16 - 1):
            rows = jnp.where(jnp.abs(zz - z - 16 * j) <= radius, rows, 0.0)
        high, low = split(rows)
        ref[16 * j : 16 * j + 16, 0:LANES] = high
        ref[16 * j : 16 * j + 16, LANES:] = low


def edges(flag, low, high):
    even = flag == 0
    return jnp.where(even, high, low), jnp.where(even, low, high)


def pieces_kernel(images_ref, axial_ref, first_ref, second_ref, out_ref, rows, taps, axial, taps_1, taps_2, taps_sems, in_sems, out_sems):
    small = [
        pltpu.make_async_copy(src, dst, taps_sems.at[k])
        for k, (src, dst) in enumerate(
            ((axial_ref, axial), (first_ref, taps_1), (second_ref, taps_2))
        )
    ]
    ins = [
        pltpu.make_async_copy(images_ref.at[i], rows.at[i], in_sems.at[i]) for i in range(ROWS)
    ]
    outs = [
        pltpu.make_async_copy(
            rows.at[i], out_ref.at[:, pl.ds(WIDTH * i, WIDTH), :], out_sems.at[i]
        )
        for i in range(ROWS)
    ]
    outs.append(pltpu.make_async_copy(taps, out_ref.at[:, pl.ds(BLOCK, 8), :], out_sems.at[ROWS]))
    for copy in small + ins:
        copy.start()
    taps[...] = jnp.zeros_like(taps)
    for copy in small:
        copy.wait()
    for row, ref in enumerate((axial, taps_1, taps_2)):
        taps[:, row : row + 1, 0 : ref.shape[1]] = jnp.broadcast_to(
            ref[...][None], (taps.shape[0], 1, ref.shape[1])
        )
    outs[ROWS].start()
    for i in range(ROWS):
        ins[i].wait()
        outs[i].start()
    for copy in outs:
        copy.wait()


def make_tables(data_ref, table_ref):
    views = data_ref.shape[0]
    lane = lax.broadcasted_iota(jnp.int32, (8, LANES), 1)
    sub = lax.broadcasted_iota(jnp.int32, (8, LANES), 0)

    def one(v, carry):
        start = 0
        for row in (1, 2):
            taps = jnp.broadcast_to(data_ref[v, BLOCK + row : BLOCK + row + 1, :], (8, LANES))
            column = jnp.sum(jnp.where(lane == sub, taps, 0.0), axis=1, keepdims=True)
            table_ref[v, start : start + 8, :] = jnp.broadcast_to(column, (8, LANES))
            start += 8
        return carry

    lax.fori_loop(0, views, one, 0, unroll=2)


def tap(table_ref, v, k):
    return jnp.broadcast_to(table_ref[v, pl.ds(k, 1), :], (8, LANES))


def conv_part(sizes, est_ref, conv_ref, table_ref, spread, prepare, finish):
    nf, ns, _ = sizes
    wide, views = est_ref.shape[0], conv_ref.shape[0]

    def row(i, carry):
        shifted = [
            [est_ref[i, k + 8 * h : k + 8 * h + 8, :] for h in range(2)] for k in range(ns)
        ]
        for v in range(views):
            taps = [tap(table_ref, v, 8 + ns - 1 - k) for k in range(ns)]
            for h in range(2):
                t = taps[0] * shifted[0][h]
                for k in range(1, ns):
                    t = t + taps[k] * shifted[k][h]
                spread[v, i, 8 * h : 8 * h + 8, :] = t
        return carry

    lax.fori_loop(0, wide, row, 0)

    def one(v, carry):
        prepare(v)
        first = [tap(table_ref, v, k) for k in range(nf)]
        out = []
        for i in range(ROWS):
            for h in range(2):
                t = first[0] * spread[v, i + nf - 1, 8 * h : 8 * h + 8, :]
                for k in range(1, nf):
                    t = t + first[k] * spread[v, i + nf - 1 - k, 8 * h : 8 * h + 8, :]
                out.append(t)
        finish(v, product(jnp.concatenate(out, axis=0), conv_ref[v]))
        return carry

    lax.fori_loop(0, views, one, 0, unroll=2)


def corr_part(sizes, flags, ratio_of, conv_ref, table_ref, spread, part_ref, near_ref, far_ref):
    nf, ns, _ = sizes
    wide, views = spread.shape[1], spread.shape[0]

    def one(v, carry):
        first = [tap(table_ref, v, k) for k in range(nf)]
        back = product_t(ratio_of(v), conv_ref[v])
        for i in range(wide):
            for h in range(2):
                t = None
                for k in range(nf):
                    j = i - (nf - 1) + k
                    if 0 <= j < ROWS:
                        at = j * WIDTH + 8 * h
                        u = first[k] * back[at : at + 8]
                        t = u if t is None else t + u
                spread[v, i, 8 * h : 8 * h + 8, :] = t
        return carry

    lax.fori_loop(0, views, one, 0, unroll=4)

    def row(i, carry):
        sums = [[None, None] for _ in range(ns)]
        for v in range(views):
            g = [spread[v, i, 8 * h : 8 * h + 8, :] for h in range(2)]
            for k in range(ns):
                t = tap(table_ref, v, 8 + ns - 1 - k)
                for h in range(2):
                    u = t * g[h]
                    sums[k][h] = u if sums[k][h] is None else sums[k][h] + u
        total = None
        for k in range(ns):
            t = jnp.concatenate(sums[k] + [jnp.zeros((8, LANES), jnp.float32)], axis=0)
            t = pltpu.roll(t, k, 0) if k else t
            total = t if total is None else total + t
        part_ref[i] = total
        return carry

    lax.fori_loop(0, wide, row, 0)
    strip = near_ref.shape[0]
    near_ref[...], far_ref[...] = edges(
        flags[0], part_ref[0:strip], part_ref[wide - strip : wide]
    )


def sides(flag, near_ref, far_ref):
    even = flag == 0
    near, far = near_ref[...], far_ref[...]
    return jnp.where(even, far, near), jnp.where(even, near, far)


def both_parts(sizes, flags, est_ref, data_ref, conv_ref, table_ref, part_ref, near_ref, far_ref, spread, ratio, prepare=lambda v: None):
    def finish(v, blurred):
        ratio[v] = data_ref[v, 0:BLOCK, :] / blurred

    conv_part(sizes, est_ref, conv_ref, table_ref, spread, prepare, finish)
    corr_part(
        sizes, flags, lambda v: ratio[v],
        conv_ref, table_ref, spread, part_ref, near_ref, far_ref,
    )


def columns_kernel(halo, flags, own_ref, yn_ref, yf_ref, out_ref, near_ref, far_ref):
    low, high = sides(flags[1], yn_ref, yf_ref)
    out_ref[:, 0:halo, :] = low[:, 8 - halo :, :]
    out_ref[:, halo : halo + WIDTH, :] = own_ref[...]
    out_ref[:, halo + WIDTH : WIDTH + 2 * halo, :] = high[:, 0:halo, :]
    out_ref[:, WIDTH + 2 * halo :, :] = jnp.zeros((ROWS, COLS - WIDTH - 2 * halo, LANES), jnp.float32)
    strip = near_ref.shape[0]
    near_ref[...], far_ref[...] = edges(flags[0], out_ref[0:strip], out_ref[ROWS - strip :])


def first_kernel(sizes, flags, own_ref, xn_ref, xf_ref, data_ref, est_ref, part_ref, near_ref, far_ref, conv_ref, table_ref, spread, ratio):
    make_tables(data_ref, table_ref)
    low, high = sides(flags[0], xn_ref, xf_ref)
    strip = low.shape[0]
    est_ref[0:strip] = low
    est_ref[strip : strip + ROWS] = own_ref[...]
    est_ref[strip + ROWS :] = high

    def prepare(v):
        banded(data_ref[v, BLOCK : BLOCK + 1, :], sizes[2] // 2, conv_ref.at[v])

    both_parts(sizes, flags, est_ref, data_ref, conv_ref, table_ref, part_ref, near_ref, far_ref, spread, ratio, prepare)


def updated(views, flags, est_ref, total_ref, yn_ref, yf_ref, new_ref):
    low, high = sides(flags[1], yn_ref, yf_ref)
    new_ref[:, 0:8, :] = est_ref[:, 0:8, :] * ((total_ref[:, 0:8, :] + low) / views)
    new_ref[:, 8:16, :] = est_ref[:, 8:16, :] * (total_ref[:, 8:16, :] / views)
    new_ref[:, 16:24, :] = est_ref[:, 16:24, :] * ((total_ref[:, 16:24, :] + high) / views)


def pass_kernel(sizes, views, flags, est_ref, total_ref, yn_ref, yf_ref, data_ref, conv_ref, table_ref, new_ref, part_ref, near_ref, far_ref, spread, ratio):
    updated(views, flags, est_ref, total_ref, yn_ref, yf_ref, new_ref)
    both_parts(sizes, flags, new_ref, data_ref, conv_ref, table_ref, part_ref, near_ref, far_ref, spread, ratio)


def rows_kernel(flags, part_ref, near_ref, far_ref, out_ref, yn_ref, yf_ref):
    strip, rows = near_ref.shape[0], out_ref.shape[0]
    skip = (part_ref.shape[0] - rows) // 2
    even = flags[0] == 0
    near, far = near_ref[...], far_ref[...]
    out_ref[0:strip] = part_ref[skip : skip + strip] + jnp.where(even, far, near)
    out_ref[strip : rows - strip] = part_ref[skip + strip : skip + rows - strip]
    out_ref[rows - strip :] = part_ref[skip + rows - strip : skip + rows] + jnp.where(even, near, far)
    yn_ref[...], yf_ref[...] = edges(flags[1], out_ref[:, 0:8, :], out_ref[:, 16:24, :])


def final_kernel(views, lo_x, lo_y, flags, est_ref, total_ref, yn_ref, yf_ref, out_ref, total):
    low, high = sides(flags[1], yn_ref, yf_ref)
    total[:, 0:8, :] = total_ref[:, 0:8, :] + low
    total[:, 8:16, :] = total_ref[:, 8:16, :]
    total[:, 16:24, :] = total_ref[:, 16:24, :] + high
    own = pl.ds(lo_y, WIDTH)
    out_ref[...] = est_ref[pl.ds(lo_x, ROWS), own, :] * (total[:, own, :] / views)


def pairs(count, start):
    out = []
    for i in range(start, count - 1, 2):
        out += [(i, i + 1), (i + 1, i)]
    return out


def swapped(near, far, axis):
    count = lax.axis_size(axis)
    far = lax.ppermute(far, axis, pairs(count, 1))
    near = lax.ppermute(near, axis, pairs(count, 0))
    return near, far


VMEM = pl.BlockSpec(memory_space=pltpu.VMEM)
SMEM = pl.BlockSpec(memory_space=pltpu.SMEM)


def call(kernel, ins, shapes, scratch=(), limit=2 << 20):
    shapes = [s if isinstance(s, jax.ShapeDtypeStruct) else jax.ShapeDtypeStruct(s, jnp.float32) for s in shapes]
    return pl.pallas_call(
        kernel,
        in_specs=[SMEM] + [VMEM] * (len(ins) - 1),
        out_specs=[VMEM] * len(shapes),
        out_shape=shapes,
        scratch_shapes=list(scratch),
        compiler_params=pltpu.CompilerParams(vmem_limit_bytes=limit),
    )(*ins)


def local(estimate, images, taps_first, taps_second, taps_axial):
    nf, ns, nz = taps_first.shape[1], taps_second.shape[1], taps_axial.shape[1]
    sizes = (nf, ns, nz)
    views = lax.axis_size("view")
    rows, cols, lanes = estimate.shape
    halo = nf - 1
    wide = rows + halo
    flags = jnp.stack(
        [lax.axis_index("tile") % 2, lax.axis_index("view") % 2]
    ).astype(jnp.int32)

    hbm = pl.BlockSpec(memory_space=pltpu.HBM)
    small = (taps_axial, taps_first, taps_second)
    data = pl.pallas_call(
        pieces_kernel,
        in_specs=[hbm] * 4,
        out_specs=hbm,
        out_shape=jax.ShapeDtypeStruct((views, rows * cols + 8, lanes), jnp.float32),
        scratch_shapes=[
            pltpu.VMEM((rows, views, cols, lanes), jnp.float32),
            pltpu.VMEM((views, 8, lanes), jnp.float32),
            *(pltpu.VMEM(x.shape, jnp.float32) for x in small),
            pltpu.SemaphoreType.DMA((3,)),
            pltpu.SemaphoreType.DMA((rows,)),
            pltpu.SemaphoreType.DMA((rows + 1,)),
        ],
        compiler_params=pltpu.CompilerParams(vmem_limit_bytes=60 << 20),
    )(images.reshape(rows, views, cols, lanes), *small)
    data = lax.all_to_all(data, "view", 0, 0, tiled=True)
    matrices = jax.ShapeDtypeStruct((views, lanes, 2 * lanes), jnp.bfloat16)

    block = (wide, COLS, lanes)
    strips = [(halo, COLS, lanes)] * (ITERS - 1) + [(halo // 2, COLS, lanes)]
    scratch = [
        pltpu.VMEM((views, wide, cols, lanes), jnp.float32),
        pltpu.VMEM((views, rows * cols, lanes), jnp.float32),
    ]

    def joined(part, near, far, count):
        shapes = [(count, width, lanes) for width in (COLS, 8, 8)]
        total, yn, yf = call(rows_kernel, (flags, part, near, far), shapes)
        yn, yf = swapped(yn, yf, "view")
        return total, yn, yf

    yn, yf = edges(flags[1], estimate[:, 0:8], estimate[:, cols - 8 :])
    yn, yf = swapped(yn, yf, "view")
    thin = (halo // 2, COLS, lanes)
    own, near, far = call(
        functools.partial(columns_kernel, ns // 2),
        (flags, estimate, yn, yf),
        ((rows, COLS, lanes), thin, thin),
    )
    near, far = swapped(near, far, "tile")
    current, part, near, far, matrix, table = call(
        functools.partial(first_kernel, sizes),
        (flags, own, near, far, data),
        (block, block, strips[0], strips[0], matrices, (views, 16, lanes)),
        scratch,
        limit=16 << 20,
    )
    for step in range(1, ITERS):
        near, far = swapped(near, far, "tile")
        total, yn, yf = joined(part, near, far, wide)
        current, part, near, far = call(
            functools.partial(pass_kernel, sizes, views),
            (flags, current, total, yn, yf, data, matrix, table),
            (block, block, strips[step], strips[step]),
            scratch,
            limit=12 << 20,
        )
    near, far = swapped(near, far, "tile")
    total, yn, yf = joined(part, near, far, rows)
    (out,) = call(
        functools.partial(final_kernel, views, nf // 2, ns // 2),
        (flags, current, total, yn, yf),
        ((rows, cols, lanes),),
        [pltpu.VMEM((rows, COLS, lanes), jnp.float32)],
    )
    return out


def solution(mesh):
    in_specs = (
        P("tile", "view", None),
        P("view", "tile", None, None),
        P("view", None),
        P("view", None),
        P("view", None),
    )
    out_specs = P("tile", "view", None)
    return jax.shard_map(local, mesh=mesh, in_specs=in_specs, out_specs=out_specs, check_vma=False)
```

```python
import functools

import jax
import jax.numpy as jnp
from jax import lax
from jax.experimental import pallas as pl
from jax.experimental.pallas import tpu as pltpu
from jax.sharding import PartitionSpec as P

ITERS = 2
LANES = 128
COLS = 24
ROWS, WIDTH = 8, 16
BLOCK = ROWS * WIDTH


def split(x):
    high = x.astype(jnp.bfloat16)
    low = (x - high.astype(jnp.float32)).astype(jnp.bfloat16)
    return high, low


def product(x, matrix):
    left = jnp.concatenate(split(x), axis=1)
    right = jnp.concatenate([matrix, matrix], axis=0)
    both = jnp.dot(left, right, preferred_element_type=jnp.float32)
    return both[:, 0:LANES] + both[:, LANES:]


def banded(row, radius, ref):
    full = jnp.broadcast_to(row, (16, LANES))
    first = pltpu.roll(full, LANES - radius, 1, stride=1, stride_axis=0)
    z = lax.broadcasted_iota(jnp.int32, (16, LANES), 0)
    zz = lax.broadcasted_iota(jnp.int32, (16, LANES), 1)
    for j in range(LANES // 16):
        rows = pltpu.roll(first, 16 * j, 1) if j else first
        if j in (0, LANES // 16 - 1):
            rows = jnp.where(jnp.abs(zz - z - 16 * j) <= radius, rows, 0.0)
        high, low = split(rows)
        ref[16 * j : 16 * j + 16, 0:LANES] = high
        ref[16 * j : 16 * j + 16, LANES:] = low


def edges(flag, low, high):
    even = flag == 0
    return jnp.where(even, high, low), jnp.where(even, low, high)


def pieces_kernel(images_ref, axial_ref, first_ref, second_ref, out_ref, rows, taps, axial, taps_1, taps_2, taps_sems, in_sems, out_sems):
    small = [
        pltpu.make_async_copy(src, dst, taps_sems.at[k])
        for k, (src, dst) in enumerate(
            ((axial_ref, axial), (first_ref, taps_1), (second_ref, taps_2))
        )
    ]
    ins = [
        pltpu.make_async_copy(images_ref.at[i], rows.at[i], in_sems.at[i]) for i in range(ROWS)
    ]
    outs = [
        pltpu.make_async_copy(
            rows.at[i], out_ref.at[:, pl.ds(WIDTH * i, WIDTH), :], out_sems.at[i]
        )
        for i in range(ROWS)
    ]
    outs.append(pltpu.make_async_copy(taps, out_ref.at[:, pl.ds(BLOCK, 8), :], out_sems.at[ROWS]))
    for copy in small + ins:
        copy.start()
    taps[...] = jnp.zeros_like(taps)
    for copy in small:
        copy.wait()
    for row, ref in enumerate((axial, taps_1, taps_2)):
        taps[:, row : row + 1, 0 : ref.shape[1]] = jnp.broadcast_to(
            ref[...][None], (taps.shape[0], 1, ref.shape[1])
        )
    outs[ROWS].start()
    for i in range(ROWS):
        ins[i].wait()
        outs[i].start()
    for copy in outs:
        copy.wait()


def make_tables(sizes, data_ref, table_ref, axial):
    _, _, nz = sizes
    views = data_ref.shape[0]
    lane = lax.broadcasted_iota(jnp.int32, (8, LANES), 1)
    sub = lax.broadcasted_iota(jnp.int32, (8, LANES), 0)
    for v in range(views):
        axial[v : v + 1, :] = data_ref[v, BLOCK : BLOCK + 1, :]
    z = lax.broadcasted_iota(jnp.int32, (LANES, LANES), 0)
    zz = lax.broadcasted_iota(jnp.int32, (LANES, LANES), 1)
    reverse = jnp.where(z + zz == nz - 1, 1.0, 0.0).astype(jnp.float32)
    axial[views:, :] = jnp.dot(
        axial[0:views, :], reverse, precision=lax.Precision.HIGHEST, preferred_element_type=jnp.float32
    )

    def one(v, carry):
        start = 0
        for row in (1, 2):
            taps = jnp.broadcast_to(data_ref[v, BLOCK + row : BLOCK + row + 1, :], (8, LANES))
            column = jnp.sum(jnp.where(lane == sub, taps, 0.0), axis=1, keepdims=True)
            table_ref[v, start : start + 8, :] = jnp.broadcast_to(column, (8, LANES))
            start += 8
        return carry

    lax.fori_loop(0, views, one, 0, unroll=2)


def tap(table_ref, v, k):
    return jnp.broadcast_to(table_ref[v, pl.ds(k, 1), :], (8, LANES))


def conv_part(sizes, est_ref, conv_ref, table_ref, spread, prepare, finish):
    nf, ns, _ = sizes
    wide, views = est_ref.shape[0], conv_ref.shape[0]

    def row(i, carry):
        shifted = [
            [est_ref[i, k + 8 * h : k + 8 * h + 8, :] for h in range(2)] for k in range(ns)
        ]
        for v in range(views):
            taps = [tap(table_ref, v, 8 + ns - 1 - k) for k in range(ns)]
            for h in range(2):
                t = taps[0] * shifted[0][h]
                for k in range(1, ns):
                    t = t + taps[k] * shifted[k][h]
                spread[v, i, 8 * h : 8 * h + 8, :] = t
        return carry

    lax.fori_loop(0, wide, row, 0)

    def one(v, carry):
        prepare(v)
        first = [tap(table_ref, v, k) for k in range(nf)]
        out = []
        for i in range(ROWS):
            for h in range(2):
                t = first[0] * spread[v, i + nf - 1, 8 * h : 8 * h + 8, :]
                for k in range(1, nf):
                    t = t + first[k] * spread[v, i + nf - 1 - k, 8 * h : 8 * h + 8, :]
                out.append(t)
        finish(v, product(jnp.concatenate(out, axis=0), conv_ref[v]))
        return carry

    lax.fori_loop(0, views, one, 0, unroll=2)


def corr_part(sizes, flags, ratio_of, corr_ref, table_ref, spread, part_ref, near_ref, far_ref, prepare):
    nf, ns, _ = sizes
    wide, views = spread.shape[1], spread.shape[0]

    def one(v, carry):
        first = [tap(table_ref, v, k) for k in range(nf)]
        prepare(v)
        back = product(ratio_of(v), corr_ref[v])
        for i in range(wide):
            for h in range(2):
                t = None
                for k in range(nf):
                    j = i - (nf - 1) + k
                    if 0 <= j < ROWS:
                        at = j * WIDTH + 8 * h
                        u = first[k] * back[at : at + 8]
                        t = u if t is None else t + u
                spread[v, i, 8 * h : 8 * h + 8, :] = t
        return carry

    lax.fori_loop(0, views, one, 0, unroll=4)

    def row(i, carry):
        sums = [[None, None] for _ in range(ns)]
        for v in range(views):
            g = [spread[v, i, 8 * h : 8 * h + 8, :] for h in range(2)]
            for k in range(ns):
                t = tap(table_ref, v, 8 + ns - 1 - k)
                for h in range(2):
                    u = t * g[h]
                    sums[k][h] = u if sums[k][h] is None else sums[k][h] + u
        total = None
        for k in range(ns):
            t = jnp.concatenate(sums[k] + [jnp.zeros((8, LANES), jnp.float32)], axis=0)
            t = pltpu.roll(t, k, 0) if k else t
            total = t if total is None else total + t
        part_ref[i] = total
        return carry

    lax.fori_loop(0, wide, row, 0)
    strip = near_ref.shape[0]
    near_ref[...], far_ref[...] = edges(
        flags[0], part_ref[0:strip], part_ref[wide - strip : wide]
    )


def sides(flag, near_ref, far_ref):
    even = flag == 0
    near, far = near_ref[...], far_ref[...]
    return jnp.where(even, far, near), jnp.where(even, near, far)


def both_parts(sizes, flags, est_ref, data_ref, conv_ref, corr_ref, table_ref, part_ref, near_ref, far_ref, spread, ratio, prepare=lambda v: None, prepare_corr=lambda v: None):
    def finish(v, blurred):
        ratio[v] = data_ref[v, 0:BLOCK, :] / blurred

    conv_part(sizes, est_ref, conv_ref, table_ref, spread, prepare, finish)
    corr_part(
        sizes, flags, lambda v: ratio[v],
        corr_ref, table_ref, spread, part_ref, near_ref, far_ref, prepare_corr,
    )


def columns_kernel(halo, flags, own_ref, yn_ref, yf_ref, out_ref, near_ref, far_ref):
    low, high = sides(flags[1], yn_ref, yf_ref)
    out_ref[:, 0:halo, :] = low[:, 8 - halo :, :]
    out_ref[:, halo : halo + WIDTH, :] = own_ref[...]
    out_ref[:, halo + WIDTH : WIDTH + 2 * halo, :] = high[:, 0:halo, :]
    out_ref[:, WIDTH + 2 * halo :, :] = jnp.zeros((ROWS, COLS - WIDTH - 2 * halo, LANES), jnp.float32)
    strip = near_ref.shape[0]
    near_ref[...], far_ref[...] = edges(flags[0], out_ref[0:strip], out_ref[ROWS - strip :])


def first_kernel(sizes, flags, own_ref, xn_ref, xf_ref, data_ref, est_ref, part_ref, near_ref, far_ref, conv_ref, corr_ref, table_ref, spread, ratio, axial):
    make_tables(sizes, data_ref, table_ref, axial)
    low, high = sides(flags[0], xn_ref, xf_ref)
    strip = low.shape[0]
    est_ref[0:strip] = low
    est_ref[strip : strip + ROWS] = own_ref[...]
    est_ref[strip + ROWS :] = high

    def prepare(v):
        banded(axial[pl.ds(v, 1), :], sizes[2] // 2, conv_ref.at[v])

    def prepare_corr(v):
        banded(axial[pl.ds(data_ref.shape[0] + v, 1), :], sizes[2] // 2, corr_ref.at[v])

    both_parts(sizes, flags, est_ref, data_ref, conv_ref, corr_ref, table_ref, part_ref, near_ref, far_ref, spread, ratio, prepare, prepare_corr)


def updated(views, flags, est_ref, total_ref, yn_ref, yf_ref, new_ref):
    low, high = sides(flags[1], yn_ref, yf_ref)
    new_ref[:, 0:8, :] = est_ref[:, 0:8, :] * ((total_ref[:, 0:8, :] + low) / views)
    new_ref[:, 8:16, :] = est_ref[:, 8:16, :] * (total_ref[:, 8:16, :] / views)
    new_ref[:, 16:24, :] = est_ref[:, 16:24, :] * ((total_ref[:, 16:24, :] + high) / views)


def pass_kernel(sizes, views, flags, est_ref, total_ref, yn_ref, yf_ref, data_ref, conv_ref, corr_ref, table_ref, new_ref, part_ref, near_ref, far_ref, spread, ratio):
    updated(views, flags, est_ref, total_ref, yn_ref, yf_ref, new_ref)
    both_parts(sizes, flags, new_ref, data_ref, conv_ref, corr_ref, table_ref, part_ref, near_ref, far_ref, spread, ratio)


def rows_kernel(flags, part_ref, near_ref, far_ref, out_ref, yn_ref, yf_ref):
    strip, rows = near_ref.shape[0], out_ref.shape[0]
    skip = (part_ref.shape[0] - rows) // 2
    even = flags[0] == 0
    near, far = near_ref[...], far_ref[...]
    out_ref[0:strip] = part_ref[skip : skip + strip] + jnp.where(even, far, near)
    out_ref[strip : rows - strip] = part_ref[skip + strip : skip + rows - strip]
    out_ref[rows - strip :] = part_ref[skip + rows - strip : skip + rows] + jnp.where(even, near, far)
    yn_ref[...], yf_ref[...] = edges(flags[1], out_ref[:, 0:8, :], out_ref[:, 16:24, :])


def final_kernel(views, lo_x, lo_y, flags, est_ref, total_ref, yn_ref, yf_ref, out_ref, total):
    low, high = sides(flags[1], yn_ref, yf_ref)
    total[:, 0:8, :] = total_ref[:, 0:8, :] + low
    total[:, 8:16, :] = total_ref[:, 8:16, :]
    total[:, 16:24, :] = total_ref[:, 16:24, :] + high
    own = pl.ds(lo_y, WIDTH)
    out_ref[...] = est_ref[pl.ds(lo_x, ROWS), own, :] * (total[:, own, :] / views)


def pairs(count, start):
    out = []
    for i in range(start, count - 1, 2):
        out += [(i, i + 1), (i + 1, i)]
    return out


def swapped(near, far, axis):
    count = lax.axis_size(axis)
    far = lax.ppermute(far, axis, pairs(count, 1))
    near = lax.ppermute(near, axis, pairs(count, 0))
    return near, far


VMEM = pl.BlockSpec(memory_space=pltpu.VMEM)
SMEM = pl.BlockSpec(memory_space=pltpu.SMEM)


def call(kernel, ins, shapes, scratch=(), limit=2 << 20):
    shapes = [s if isinstance(s, jax.ShapeDtypeStruct) else jax.ShapeDtypeStruct(s, jnp.float32) for s in shapes]
    return pl.pallas_call(
        kernel,
        in_specs=[SMEM] + [VMEM] * (len(ins) - 1),
        out_specs=[VMEM] * len(shapes),
        out_shape=shapes,
        scratch_shapes=list(scratch),
        compiler_params=pltpu.CompilerParams(vmem_limit_bytes=limit),
    )(*ins)


def local(estimate, images, taps_first, taps_second, taps_axial):
    nf, ns, nz = taps_first.shape[1], taps_second.shape[1], taps_axial.shape[1]
    sizes = (nf, ns, nz)
    views = lax.axis_size("view")
    rows, cols, lanes = estimate.shape
    halo = nf - 1
    wide = rows + halo
    flags = jnp.stack(
        [lax.axis_index("tile") % 2, lax.axis_index("view") % 2]
    ).astype(jnp.int32)

    hbm = pl.BlockSpec(memory_space=pltpu.HBM)
    small = (taps_axial, taps_first, taps_second)
    data = pl.pallas_call(
        pieces_kernel,
        in_specs=[hbm] * 4,
        out_specs=hbm,
        out_shape=jax.ShapeDtypeStruct((views, rows * cols + 8, lanes), jnp.float32),
        scratch_shapes=[
            pltpu.VMEM((rows, views, cols, lanes), jnp.float32),
            pltpu.VMEM((views, 8, lanes), jnp.float32),
            *(pltpu.VMEM(x.shape, jnp.float32) for x in small),
            pltpu.SemaphoreType.DMA((3,)),
            pltpu.SemaphoreType.DMA((rows,)),
            pltpu.SemaphoreType.DMA((rows + 1,)),
        ],
        compiler_params=pltpu.CompilerParams(vmem_limit_bytes=60 << 20),
    )(images.reshape(rows, views, cols, lanes), *small)
    data = lax.all_to_all(data, "view", 0, 0, tiled=True)
    matrices = jax.ShapeDtypeStruct((views, lanes, 2 * lanes), jnp.bfloat16)

    block = (wide, COLS, lanes)
    strips = [(halo, COLS, lanes)] * (ITERS - 1) + [(halo // 2, COLS, lanes)]
    scratch = [
        pltpu.VMEM((views, wide, cols, lanes), jnp.float32),
        pltpu.VMEM((views, rows * cols, lanes), jnp.float32),
    ]

    def joined(part, near, far, count):
        shapes = [(count, width, lanes) for width in (COLS, 8, 8)]
        total, yn, yf = call(rows_kernel, (flags, part, near, far), shapes)
        yn, yf = swapped(yn, yf, "view")
        return total, yn, yf

    yn, yf = edges(flags[1], estimate[:, 0:8], estimate[:, cols - 8 :])
    yn, yf = swapped(yn, yf, "view")
    thin = (halo // 2, COLS, lanes)
    own, near, far = call(
        functools.partial(columns_kernel, ns // 2),
        (flags, estimate, yn, yf),
        ((rows, COLS, lanes), thin, thin),
    )
    near, far = swapped(near, far, "tile")
    current, part, near, far, conv, corr, table = call(
        functools.partial(first_kernel, sizes),
        (flags, own, near, far, data),
        (block, block, strips[0], strips[0], matrices, matrices, (views, 16, lanes)),
        scratch + [pltpu.VMEM((2 * views, lanes), jnp.float32)],
        limit=16 << 20,
    )
    for step in range(1, ITERS):
        near, far = swapped(near, far, "tile")
        total, yn, yf = joined(part, near, far, wide)
        current, part, near, far = call(
            functools.partial(pass_kernel, sizes, views),
            (flags, current, total, yn, yf, data, conv, corr, table),
            (block, block, strips[step], strips[step]),
            scratch,
            limit=12 << 20,
        )
    near, far = swapped(near, far, "tile")
    total, yn, yf = joined(part, near, far, rows)
    (out,) = call(
        functools.partial(final_kernel, views, nf // 2, ns // 2),
        (flags, current, total, yn, yf),
        ((rows, cols, lanes),),
        [pltpu.VMEM((rows, COLS, lanes), jnp.float32)],
    )
    return out


def solution(mesh):
    in_specs = (
        P("tile", "view", None),
        P("view", "tile", None, None),
        P("view", None),
        P("view", None),
        P("view", None),
    )
    out_specs = P("tile", "view", None)
    return jax.shard_map(local, mesh=mesh, in_specs=in_specs, out_specs=out_specs, check_vma=False)
```

```python
import functools

import jax
import jax.numpy as jnp
from jax import lax
from jax.experimental import pallas as pl
from jax.experimental.pallas import tpu as pltpu
from jax.sharding import PartitionSpec as P

ITERS = 2
LANES = 128
COLS = 24
ROWS, WIDTH = 8, 16
BLOCK = ROWS * WIDTH


def split(x):
    high = x.astype(jnp.bfloat16)
    low = (x - high.astype(jnp.float32)).astype(jnp.bfloat16)
    return high, low


def product(x, matrix):
    left = jnp.concatenate(split(x), axis=1)
    right = jnp.concatenate([matrix, matrix], axis=0)
    both = jnp.dot(left, right, preferred_element_type=jnp.float32)
    return both[:, 0:LANES] + both[:, LANES:]


def banded(row, radius, ref):
    full = jnp.broadcast_to(row, (16, LANES))
    first = pltpu.roll(full, LANES - radius, 1, stride=1, stride_axis=0)
    z = lax.broadcasted_iota(jnp.int32, (16, LANES), 0)
    zz = lax.broadcasted_iota(jnp.int32, (16, LANES), 1)
    for j in range(LANES // 16):
        rows = pltpu.roll(first, 16 * j, 1) if j else first
        if j in (0, LANES // 16 - 1):
            rows = jnp.where(jnp.abs(zz - z - 16 * j) <= radius, rows, 0.0)
        high, low = split(rows)
        ref[16 * j : 16 * j + 16, 0:LANES] = high
        ref[16 * j : 16 * j + 16, LANES:] = low


def edges(flag, low, high):
    even = flag == 0
    return jnp.where(even, high, low), jnp.where(even, low, high)


def pieces_kernel(images_ref, axial_ref, first_ref, second_ref, out_ref, rows, taps, axial, taps_1, taps_2, taps_sems, in_sems, out_sems):
    small = [
        pltpu.make_async_copy(src, dst, taps_sems.at[k])
        for k, (src, dst) in enumerate(
            ((axial_ref, axial), (first_ref, taps_1), (second_ref, taps_2))
        )
    ]
    ins = [
        pltpu.make_async_copy(images_ref.at[i], rows.at[i], in_sems.at[i]) for i in range(ROWS)
    ]
    outs = [
        pltpu.make_async_copy(
            rows.at[i], out_ref.at[:, pl.ds(WIDTH * i, WIDTH), :], out_sems.at[i]
        )
        for i in range(ROWS)
    ]
    outs.append(pltpu.make_async_copy(taps, out_ref.at[:, pl.ds(BLOCK, 8), :], out_sems.at[ROWS]))
    for copy in small + ins:
        copy.start()
    taps[...] = jnp.zeros_like(taps)
    for copy in small:
        copy.wait()
    for row, ref in enumerate((axial, taps_1, taps_2)):
        taps[:, row : row + 1, 0 : ref.shape[1]] = jnp.broadcast_to(
            ref[...][None], (taps.shape[0], 1, ref.shape[1])
        )
    outs[ROWS].start()
    for i in range(ROWS):
        ins[i].wait()
        outs[i].start()
    for copy in outs:
        copy.wait()


def make_tables(sizes, data_ref, table_ref, axial):
    _, _, nz = sizes
    views = data_ref.shape[0]
    lane = lax.broadcasted_iota(jnp.int32, (8, LANES), 1)
    sub = lax.broadcasted_iota(jnp.int32, (8, LANES), 0)
    for v in range(views):
        axial[v : v + 1, :] = data_ref[v, BLOCK : BLOCK + 1, :]
    z = lax.broadcasted_iota(jnp.int32, (LANES, LANES), 0)
    zz = lax.broadcasted_iota(jnp.int32, (LANES, LANES), 1)
    reverse = jnp.where(z + zz == nz - 1, 1.0, 0.0).astype(jnp.float32)
    axial[views:, :] = jnp.dot(
        axial[0:views, :], reverse, precision=lax.Precision.HIGHEST, preferred_element_type=jnp.float32
    )

    def one(v, carry):
        start = 0
        for row in (1, 2):
            taps = jnp.broadcast_to(data_ref[v, BLOCK + row : BLOCK + row + 1, :], (8, LANES))
            column = jnp.sum(jnp.where(lane == sub, taps, 0.0), axis=1, keepdims=True)
            table_ref[v, start : start + 8, :] = jnp.broadcast_to(column, (8, LANES))
            start += 8
        return carry

    lax.fori_loop(0, views, one, 0, unroll=2)


def tap(table_ref, v, k):
    return jnp.broadcast_to(table_ref[v, pl.ds(k, 1), :], (8, LANES))


def conv_part(sizes, est_ref, conv_ref, table_ref, spread, prepare, finish):
    nf, ns, _ = sizes
    wide, views = est_ref.shape[0], conv_ref.shape[0]

    def row(i, carry):
        shifted = [
            [est_ref[i, k + 8 * h : k + 8 * h + 8, :] for h in range(2)] for k in range(ns)
        ]
        for v in range(views):
            taps = [tap(table_ref, v, 8 + ns - 1 - k) for k in range(ns)]
            for h in range(2):
                t = taps[0] * shifted[0][h]
                for k in range(1, ns):
                    t = t + taps[k] * shifted[k][h]
                spread[v, i, 8 * h : 8 * h + 8, :] = t
        return carry

    lax.fori_loop(0, wide, row, 0)

    def one(v, carry):
        prepare(v)
        first = [tap(table_ref, v, k) for k in range(nf)]
        out = []
        for i in range(ROWS):
            for h in range(2):
                t = first[0] * spread[v, i + nf - 1, 8 * h : 8 * h + 8, :]
                for k in range(1, nf):
                    t = t + first[k] * spread[v, i + nf - 1 - k, 8 * h : 8 * h + 8, :]
                out.append(t)
        finish(v, product(jnp.concatenate(out, axis=0), conv_ref[v]))
        return carry

    lax.fori_loop(0, views, one, 0, unroll=2)


def corr_part(sizes, flags, ratio_of, corr_ref, table_ref, spread, part_ref, near_ref, far_ref, prepare):
    nf, ns, _ = sizes
    wide, views = spread.shape[1], spread.shape[0]

    def one(v, carry):
        first = [tap(table_ref, v, k) for k in range(nf)]
        prepare(v)
        back = product(ratio_of(v), corr_ref[v])
        for i in range(wide):
            for h in range(2):
                t = None
                for k in range(nf):
                    j = i - (nf - 1) + k
                    if 0 <= j < ROWS:
                        at = j * WIDTH + 8 * h
                        u = first[k] * back[at : at + 8]
                        t = u if t is None else t + u
                spread[v, i, 8 * h : 8 * h + 8, :] = t
        return carry

    lax.fori_loop(0, views, one, 0, unroll=4)

    def row(i, carry):
        sums = [[None, None] for _ in range(ns)]
        for v in range(views):
            g = [spread[v, i, 8 * h : 8 * h + 8, :] for h in range(2)]
            for k in range(ns):
                t = tap(table_ref, v, 8 + ns - 1 - k)
                for h in range(2):
                    u = t * g[h]
                    sums[k][h] = u if sums[k][h] is None else sums[k][h] + u
        total = None
        for k in range(ns):
            t = jnp.concatenate(sums[k] + [jnp.zeros((8, LANES), jnp.float32)], axis=0)
            t = pltpu.roll(t, k, 0) if k else t
            total = t if total is None else total + t
        part_ref[i] = total
        return carry

    lax.fori_loop(0, wide, row, 0)
    strip = near_ref.shape[0]
    near_ref[...], far_ref[...] = edges(
        flags[0], part_ref[0:strip], part_ref[wide - strip : wide]
    )


def sides(flag, near_ref, far_ref):
    even = flag == 0
    near, far = near_ref[...], far_ref[...]
    return jnp.where(even, far, near), jnp.where(even, near, far)


def both_parts(sizes, flags, est_ref, data_ref, conv_ref, corr_ref, table_ref, part_ref, near_ref, far_ref, spread, ratio, prepare=lambda v: None, prepare_corr=lambda v: None):
    def finish(v, blurred):
        ratio[v] = data_ref[v, 0:BLOCK, :] / blurred

    conv_part(sizes, est_ref, conv_ref, table_ref, spread, prepare, finish)
    corr_part(
        sizes, flags, lambda v: ratio[v],
        corr_ref, table_ref, spread, part_ref, near_ref, far_ref, prepare_corr,
    )


def columns_kernel(halo, flags, own_ref, yn_ref, yf_ref, out_ref, near_ref, far_ref):
    low, high = sides(flags[1], yn_ref, yf_ref)
    out_ref[:, 0:halo, :] = low[:, WIDTH - halo :, :]
    out_ref[:, halo : halo + WIDTH, :] = own_ref[...]
    out_ref[:, halo + WIDTH : WIDTH + 2 * halo, :] = high[:, 0:halo, :]
    out_ref[:, WIDTH + 2 * halo :, :] = jnp.zeros((ROWS, COLS - WIDTH - 2 * halo, LANES), jnp.float32)
    strip = near_ref.shape[0]
    near_ref[...], far_ref[...] = edges(flags[0], out_ref[0:strip], out_ref[ROWS - strip :])


def first_kernel(sizes, flags, own_ref, xn_ref, xf_ref, data_ref, est_ref, part_ref, near_ref, far_ref, conv_ref, corr_ref, table_ref, spread, ratio, axial):
    make_tables(sizes, data_ref, table_ref, axial)
    low, high = sides(flags[0], xn_ref, xf_ref)
    strip = low.shape[0]
    est_ref[0:strip] = low
    est_ref[strip : strip + ROWS] = own_ref[...]
    est_ref[strip + ROWS :] = high

    def prepare(v):
        banded(axial[pl.ds(v, 1), :], sizes[2] // 2, conv_ref.at[v])

    def prepare_corr(v):
        banded(axial[pl.ds(data_ref.shape[0] + v, 1), :], sizes[2] // 2, corr_ref.at[v])

    both_parts(sizes, flags, est_ref, data_ref, conv_ref, corr_ref, table_ref, part_ref, near_ref, far_ref, spread, ratio, prepare, prepare_corr)


def updated(views, flags, est_ref, total_ref, yn_ref, yf_ref, new_ref):
    low, high = sides(flags[1], yn_ref, yf_ref)
    new_ref[:, 0:8, :] = est_ref[:, 0:8, :] * ((total_ref[:, 0:8, :] + low) / views)
    new_ref[:, 8:16, :] = est_ref[:, 8:16, :] * (total_ref[:, 8:16, :] / views)
    new_ref[:, 16:24, :] = est_ref[:, 16:24, :] * ((total_ref[:, 16:24, :] + high) / views)


def pass_kernel(sizes, views, flags, est_ref, total_ref, yn_ref, yf_ref, data_ref, conv_ref, corr_ref, table_ref, new_ref, part_ref, near_ref, far_ref, spread, ratio):
    updated(views, flags, est_ref, total_ref, yn_ref, yf_ref, new_ref)
    both_parts(sizes, flags, new_ref, data_ref, conv_ref, corr_ref, table_ref, part_ref, near_ref, far_ref, spread, ratio)


def rows_kernel(flags, part_ref, near_ref, far_ref, out_ref, yn_ref, yf_ref):
    strip, rows = near_ref.shape[0], out_ref.shape[0]
    skip = (part_ref.shape[0] - rows) // 2
    even = flags[0] == 0
    near, far = near_ref[...], far_ref[...]
    out_ref[0:strip] = part_ref[skip : skip + strip] + jnp.where(even, far, near)
    out_ref[strip : rows - strip] = part_ref[skip + strip : skip + rows - strip]
    out_ref[rows - strip :] = part_ref[skip + rows - strip : skip + rows] + jnp.where(even, near, far)
    yn_ref[...], yf_ref[...] = edges(flags[1], out_ref[:, 0:8, :], out_ref[:, 16:24, :])


def final_kernel(views, lo_x, lo_y, flags, est_ref, total_ref, yn_ref, yf_ref, out_ref, total):
    low, high = sides(flags[1], yn_ref, yf_ref)
    total[:, 0:8, :] = total_ref[:, 0:8, :] + low
    total[:, 8:16, :] = total_ref[:, 8:16, :]
    total[:, 16:24, :] = total_ref[:, 16:24, :] + high
    own = pl.ds(lo_y, WIDTH)
    out_ref[...] = est_ref[pl.ds(lo_x, ROWS), own, :] * (total[:, own, :] / views)


def pairs(count, start):
    out = []
    for i in range(start, count - 1, 2):
        out += [(i, i + 1), (i + 1, i)]
    return out


def swapped(near, far, axis):
    count = lax.axis_size(axis)
    far = lax.ppermute(far, axis, pairs(count, 1))
    near = lax.ppermute(near, axis, pairs(count, 0))
    return near, far


VMEM = pl.BlockSpec(memory_space=pltpu.VMEM)
SMEM = pl.BlockSpec(memory_space=pltpu.SMEM)


def call(kernel, ins, shapes, scratch=(), limit=2 << 20):
    shapes = [s if isinstance(s, jax.ShapeDtypeStruct) else jax.ShapeDtypeStruct(s, jnp.float32) for s in shapes]
    return pl.pallas_call(
        kernel,
        in_specs=[SMEM] + [VMEM] * (len(ins) - 1),
        out_specs=[VMEM] * len(shapes),
        out_shape=shapes,
        scratch_shapes=list(scratch),
        compiler_params=pltpu.CompilerParams(vmem_limit_bytes=limit),
    )(*ins)


def local(estimate, images, taps_first, taps_second, taps_axial):
    nf, ns, nz = taps_first.shape[1], taps_second.shape[1], taps_axial.shape[1]
    sizes = (nf, ns, nz)
    views = lax.axis_size("view")
    rows, cols, lanes = estimate.shape
    halo = nf - 1
    wide = rows + halo
    flags = jnp.stack(
        [lax.axis_index("tile") % 2, lax.axis_index("view") % 2]
    ).astype(jnp.int32)

    hbm = pl.BlockSpec(memory_space=pltpu.HBM)
    small = (taps_axial, taps_first, taps_second)
    data = pl.pallas_call(
        pieces_kernel,
        in_specs=[hbm] * 4,
        out_specs=hbm,
        out_shape=jax.ShapeDtypeStruct((views, rows * cols + 8, lanes), jnp.float32),
        scratch_shapes=[
            pltpu.VMEM((rows, views, cols, lanes), jnp.float32),
            pltpu.VMEM((views, 8, lanes), jnp.float32),
            *(pltpu.VMEM(x.shape, jnp.float32) for x in small),
            pltpu.SemaphoreType.DMA((3,)),
            pltpu.SemaphoreType.DMA((rows,)),
            pltpu.SemaphoreType.DMA((rows + 1,)),
        ],
        compiler_params=pltpu.CompilerParams(vmem_limit_bytes=60 << 20),
    )(images.reshape(rows, views, cols, lanes), *small)
    data = lax.all_to_all(data, "view", 0, 0, tiled=True)
    matrices = jax.ShapeDtypeStruct((views, lanes, 2 * lanes), jnp.bfloat16)

    block = (wide, COLS, lanes)
    strips = [(halo, COLS, lanes)] * (ITERS - 1) + [(halo // 2, COLS, lanes)]
    scratch = [
        pltpu.VMEM((views, wide, cols, lanes), jnp.float32),
        pltpu.VMEM((views, rows * cols, lanes), jnp.float32),
    ]

    def joined(part, near, far, count):
        shapes = [(count, width, lanes) for width in (COLS, 8, 8)]
        total, yn, yf = call(rows_kernel, (flags, part, near, far), shapes)
        yn, yf = swapped(yn, yf, "view")
        return total, yn, yf

    yn, yf = swapped(estimate, estimate, "view")
    thin = (halo // 2, COLS, lanes)
    own, near, far = call(
        functools.partial(columns_kernel, ns // 2),
        (flags, estimate, yn, yf),
        ((rows, COLS, lanes), thin, thin),
    )
    near, far = swapped(near, far, "tile")
    current, part, near, far, conv, corr, table = call(
        functools.partial(first_kernel, sizes),
        (flags, own, near, far, data),
        (block, block, strips[0], strips[0], matrices, matrices, (views, 16, lanes)),
        scratch + [pltpu.VMEM((2 * views, lanes), jnp.float32)],
        limit=16 << 20,
    )
    for step in range(1, ITERS):
        near, far = swapped(near, far, "tile")
        total, yn, yf = joined(part, near, far, wide)
        current, part, near, far = call(
            functools.partial(pass_kernel, sizes, views),
            (flags, current, total, yn, yf, data, conv, corr, table),
            (block, block, strips[step], strips[step]),
            scratch,
            limit=12 << 20,
        )
    near, far = swapped(near, far, "tile")
    total, yn, yf = joined(part, near, far, rows)
    (out,) = call(
        functools.partial(final_kernel, views, nf // 2, ns // 2),
        (flags, current, total, yn, yf),
        ((rows, cols, lanes),),
        [pltpu.VMEM((rows, COLS, lanes), jnp.float32)],
    )
    return out


def solution(mesh):
    in_specs = (
        P("tile", "view", None),
        P("view", "tile", None, None),
        P("view", None),
        P("view", None),
        P("view", None),
    )
    out_specs = P("tile", "view", None)
    return jax.shard_map(local, mesh=mesh, in_specs=in_specs, out_specs=out_specs, check_vma=False)
```

```python
import functools

import jax
import jax.numpy as jnp
from jax import lax
from jax.experimental import pallas as pl
from jax.experimental.pallas import tpu as pltpu
from jax.sharding import PartitionSpec as P

ITERS = 2
LANES = 128
COLS = 24
ROWS, WIDTH = 8, 16
BLOCK = ROWS * WIDTH


def split(x):
    high = x.astype(jnp.bfloat16)
    low = (x - high.astype(jnp.float32)).astype(jnp.bfloat16)
    return high, low


def product(x, matrix):
    left = jnp.concatenate(split(x), axis=1)
    right = jnp.concatenate([matrix, matrix], axis=0)
    both = jnp.dot(left, right, preferred_element_type=jnp.float32)
    return both[:, 0:LANES] + both[:, LANES:]


def banded(row, radius, ref):
    full = jnp.broadcast_to(row, (16, LANES))
    first = pltpu.roll(full, LANES - radius, 1, stride=1, stride_axis=0)
    z = lax.broadcasted_iota(jnp.int32, (16, LANES), 0)
    zz = lax.broadcasted_iota(jnp.int32, (16, LANES), 1)
    for j in range(LANES // 16):
        rows = pltpu.roll(first, 16 * j, 1) if j else first
        if j in (0, LANES // 16 - 1):
            rows = jnp.where(jnp.abs(zz - z - 16 * j) <= radius, rows, 0.0)
        high, low = split(rows)
        ref[16 * j : 16 * j + 16, 0:LANES] = high
        ref[16 * j : 16 * j + 16, LANES:] = low


def edges(flag, low, high):
    even = flag == 0
    return jnp.where(even, high, low), jnp.where(even, low, high)


def pieces_kernel(images_ref, axial_ref, first_ref, second_ref, out_ref, rows, taps, axial, taps_1, taps_2, taps_sems, in_sems, out_sems):
    small = [
        pltpu.make_async_copy(src, dst, taps_sems.at[k])
        for k, (src, dst) in enumerate(
            ((axial_ref, axial), (first_ref, taps_1), (second_ref, taps_2))
        )
    ]
    ins = [
        pltpu.make_async_copy(images_ref.at[i], rows.at[i], in_sems.at[i]) for i in range(ROWS)
    ]
    outs = [
        pltpu.make_async_copy(
            rows.at[i], out_ref.at[:, pl.ds(WIDTH * i, WIDTH), :], out_sems.at[i]
        )
        for i in range(ROWS)
    ]
    outs.append(pltpu.make_async_copy(taps, out_ref.at[:, pl.ds(BLOCK, 8), :], out_sems.at[ROWS]))
    for copy in small + ins:
        copy.start()
    taps[...] = jnp.zeros_like(taps)
    for copy in small:
        copy.wait()
    for row, ref in enumerate((axial, taps_1, taps_2)):
        taps[:, row : row + 1, 0 : ref.shape[1]] = jnp.broadcast_to(
            ref[...][None], (taps.shape[0], 1, ref.shape[1])
        )
    outs[ROWS].start()
    for i in range(ROWS):
        ins[i].wait()
        outs[i].start()
    for copy in outs:
        copy.wait()


def make_tables(sizes, data_ref, conv_ref, corr_ref, table_ref, axial):
    _, _, nz = sizes
    views = data_ref.shape[0]
    lane = lax.broadcasted_iota(jnp.int32, (8, LANES), 1)
    sub = lax.broadcasted_iota(jnp.int32, (8, LANES), 0)
    for v in range(views):
        axial[v : v + 1, :] = data_ref[v, BLOCK : BLOCK + 1, :]
    z = lax.broadcasted_iota(jnp.int32, (LANES, LANES), 0)
    zz = lax.broadcasted_iota(jnp.int32, (LANES, LANES), 1)
    reverse = jnp.where(z + zz == nz - 1, 1.0, 0.0).astype(jnp.float32)
    axial[views:, :] = jnp.dot(
        axial[0:views, :], reverse, precision=lax.Precision.HIGHEST, preferred_element_type=jnp.float32
    )

    def one(v, carry):
        for at, ref in ((0, conv_ref), (views, corr_ref)):
            banded(axial[pl.ds(at + v, 1), :], nz // 2, ref.at[v])
        start = 0
        for row in (1, 2):
            taps = jnp.broadcast_to(data_ref[v, BLOCK + row : BLOCK + row + 1, :], (8, LANES))
            column = jnp.sum(jnp.where(lane == sub, taps, 0.0), axis=1, keepdims=True)
            table_ref[v, start : start + 8, :] = jnp.broadcast_to(column, (8, LANES))
            start += 8
        return carry

    lax.fori_loop(0, views, one, 0, unroll=2)


def tap(table_ref, v, k):
    return jnp.broadcast_to(table_ref[v, pl.ds(k, 1), :], (8, LANES))


def conv_part(sizes, est_ref, conv_ref, table_ref, spread, finish):
    nf, ns, _ = sizes
    wide, views = est_ref.shape[0], conv_ref.shape[0]

    def row(i, carry):
        shifted = [
            [est_ref[i, k + 8 * h : k + 8 * h + 8, :] for h in range(2)] for k in range(ns)
        ]
        for v in range(views):
            taps = [tap(table_ref, v, 8 + ns - 1 - k) for k in range(ns)]
            for h in range(2):
                t = taps[0] * shifted[0][h]
                for k in range(1, ns):
                    t = t + taps[k] * shifted[k][h]
                spread[v, i, 8 * h : 8 * h + 8, :] = t
        return carry

    lax.fori_loop(0, wide, row, 0)

    def one(v, carry):
        first = [tap(table_ref, v, k) for k in range(nf)]
        out = []
        for i in range(ROWS):
            for h in range(2):
                t = first[0] * spread[v, i + nf - 1, 8 * h : 8 * h + 8, :]
                for k in range(1, nf):
                    t = t + first[k] * spread[v, i + nf - 1 - k, 8 * h : 8 * h + 8, :]
                out.append(t)
        finish(v, product(jnp.concatenate(out, axis=0), conv_ref[v]))
        return carry

    lax.fori_loop(0, views, one, 0, unroll=2)


def corr_part(sizes, flags, ratio_of, corr_ref, table_ref, spread, part_ref, near_ref, far_ref):
    nf, ns, _ = sizes
    wide, views = spread.shape[1], spread.shape[0]

    def one(v, carry):
        first = [tap(table_ref, v, k) for k in range(nf)]
        back = product(ratio_of(v), corr_ref[v])
        for i in range(wide):
            for h in range(2):
                t = None
                for k in range(nf):
                    j = i - (nf - 1) + k
                    if 0 <= j < ROWS:
                        at = j * WIDTH + 8 * h
                        u = first[k] * back[at : at + 8]
                        t = u if t is None else t + u
                spread[v, i, 8 * h : 8 * h + 8, :] = t
        return carry

    lax.fori_loop(0, views, one, 0, unroll=4)

    def row(i, carry):
        sums = [[None, None] for _ in range(ns)]
        for v in range(views):
            g = [spread[v, i, 8 * h : 8 * h + 8, :] for h in range(2)]
            for k in range(ns):
                t = tap(table_ref, v, 8 + ns - 1 - k)
                for h in range(2):
                    u = t * g[h]
                    sums[k][h] = u if sums[k][h] is None else sums[k][h] + u
        total = None
        for k in range(ns):
            t = jnp.concatenate(sums[k] + [jnp.zeros((8, LANES), jnp.float32)], axis=0)
            t = pltpu.roll(t, k, 0) if k else t
            total = t if total is None else total + t
        part_ref[i] = total
        return carry

    lax.fori_loop(0, wide, row, 0)
    strip = near_ref.shape[0]
    near_ref[...], far_ref[...] = edges(
        flags[0], part_ref[0:strip], part_ref[wide - strip : wide]
    )


def sides(flag, near_ref, far_ref):
    even = flag == 0
    near, far = near_ref[...], far_ref[...]
    return jnp.where(even, far, near), jnp.where(even, near, far)


def both_parts(sizes, flags, est_ref, data_ref, conv_ref, corr_ref, table_ref, part_ref, near_ref, far_ref, spread, ratio):
    def finish(v, blurred):
        ratio[v] = data_ref[v, 0:BLOCK, :] / blurred

    conv_part(sizes, est_ref, conv_ref, table_ref, spread, finish)
    corr_part(
        sizes, flags, lambda v: ratio[v],
        corr_ref, table_ref, spread, part_ref, near_ref, far_ref,
    )


def columns_kernel(halo, flags, own_ref, yn_ref, yf_ref, out_ref, near_ref, far_ref):
    low, high = sides(flags[1], yn_ref, yf_ref)
    out_ref[:, 0:halo, :] = low[:, WIDTH - halo :, :]
    out_ref[:, halo : halo + WIDTH, :] = own_ref[...]
    out_ref[:, halo + WIDTH : WIDTH + 2 * halo, :] = high[:, 0:halo, :]
    out_ref[:, WIDTH + 2 * halo :, :] = jnp.zeros((ROWS, COLS - WIDTH - 2 * halo, LANES), jnp.float32)
    strip = near_ref.shape[0]
    near_ref[...], far_ref[...] = edges(flags[0], out_ref[0:strip], out_ref[ROWS - strip :])


def first_kernel(sizes, flags, own_ref, xn_ref, xf_ref, data_ref, est_ref, part_ref, near_ref, far_ref, conv_ref, corr_ref, table_ref, spread, ratio, axial):
    make_tables(sizes, data_ref, conv_ref, corr_ref, table_ref, axial)
    low, high = sides(flags[0], xn_ref, xf_ref)
    strip = low.shape[0]
    est_ref[0:strip] = low
    est_ref[strip : strip + ROWS] = own_ref[...]
    est_ref[strip + ROWS :] = high
    both_parts(sizes, flags, est_ref, data_ref, conv_ref, corr_ref, table_ref, part_ref, near_ref, far_ref, spread, ratio)


def updated(views, flags, est_ref, total_ref, yn_ref, yf_ref, new_ref):
    low, high = sides(flags[1], yn_ref, yf_ref)
    new_ref[:, 0:8, :] = est_ref[:, 0:8, :] * ((total_ref[:, 0:8, :] + low) / views)
    new_ref[:, 8:16, :] = est_ref[:, 8:16, :] * (total_ref[:, 8:16, :] / views)
    new_ref[:, 16:24, :] = est_ref[:, 16:24, :] * ((total_ref[:, 16:24, :] + high) / views)


def pass_kernel(sizes, views, flags, est_ref, total_ref, yn_ref, yf_ref, data_ref, conv_ref, corr_ref, table_ref, new_ref, part_ref, near_ref, far_ref, spread, ratio):
    updated(views, flags, est_ref, total_ref, yn_ref, yf_ref, new_ref)
    both_parts(sizes, flags, new_ref, data_ref, conv_ref, corr_ref, table_ref, part_ref, near_ref, far_ref, spread, ratio)


def rows_kernel(flags, part_ref, near_ref, far_ref, out_ref, yn_ref, yf_ref):
    strip, rows = near_ref.shape[0], out_ref.shape[0]
    skip = (part_ref.shape[0] - rows) // 2
    even = flags[0] == 0
    near, far = near_ref[...], far_ref[...]
    out_ref[0:strip] = part_ref[skip : skip + strip] + jnp.where(even, far, near)
    out_ref[strip : rows - strip] = part_ref[skip + strip : skip + rows - strip]
    out_ref[rows - strip :] = part_ref[skip + rows - strip : skip + rows] + jnp.where(even, near, far)
    yn_ref[...], yf_ref[...] = edges(flags[1], out_ref[:, 0:8, :], out_ref[:, 16:24, :])


def final_kernel(views, lo_x, lo_y, flags, est_ref, total_ref, yn_ref, yf_ref, out_ref, total):
    low, high = sides(flags[1], yn_ref, yf_ref)
    total[:, 0:8, :] = total_ref[:, 0:8, :] + low
    total[:, 8:16, :] = total_ref[:, 8:16, :]
    total[:, 16:24, :] = total_ref[:, 16:24, :] + high
    own = pl.ds(lo_y, WIDTH)
    out_ref[...] = est_ref[pl.ds(lo_x, ROWS), own, :] * (total[:, own, :] / views)


def pairs(count, start):
    out = []
    for i in range(start, count - 1, 2):
        out += [(i, i + 1), (i + 1, i)]
    return out


def swapped(near, far, axis):
    count = lax.axis_size(axis)
    far = lax.ppermute(far, axis, pairs(count, 1))
    near = lax.ppermute(near, axis, pairs(count, 0))
    return near, far


VMEM = pl.BlockSpec(memory_space=pltpu.VMEM)
SMEM = pl.BlockSpec(memory_space=pltpu.SMEM)


def call(kernel, ins, shapes, scratch=(), limit=2 << 20):
    shapes = [s if isinstance(s, jax.ShapeDtypeStruct) else jax.ShapeDtypeStruct(s, jnp.float32) for s in shapes]
    return pl.pallas_call(
        kernel,
        in_specs=[SMEM] + [VMEM] * (len(ins) - 1),
        out_specs=[VMEM] * len(shapes),
        out_shape=shapes,
        scratch_shapes=list(scratch),
        compiler_params=pltpu.CompilerParams(vmem_limit_bytes=limit),
    )(*ins)


def local(estimate, images, taps_first, taps_second, taps_axial):
    nf, ns, nz = taps_first.shape[1], taps_second.shape[1], taps_axial.shape[1]
    sizes = (nf, ns, nz)
    views = lax.axis_size("view")
    rows, cols, lanes = estimate.shape
    halo = nf - 1
    wide = rows + halo
    flags = jnp.stack(
        [lax.axis_index("tile") % 2, lax.axis_index("view") % 2]
    ).astype(jnp.int32)

    hbm = pl.BlockSpec(memory_space=pltpu.HBM)
    small = (taps_axial, taps_first, taps_second)
    data = pl.pallas_call(
        pieces_kernel,
        in_specs=[hbm] * 4,
        out_specs=hbm,
        out_shape=jax.ShapeDtypeStruct((views, rows * cols + 8, lanes), jnp.float32),
        scratch_shapes=[
            pltpu.VMEM((rows, views, cols, lanes), jnp.float32),
            pltpu.VMEM((views, 8, lanes), jnp.float32),
            *(pltpu.VMEM(x.shape, jnp.float32) for x in small),
            pltpu.SemaphoreType.DMA((3,)),
            pltpu.SemaphoreType.DMA((rows,)),
            pltpu.SemaphoreType.DMA((rows + 1,)),
        ],
        compiler_params=pltpu.CompilerParams(vmem_limit_bytes=60 << 20),
    )(images.reshape(rows, views, cols, lanes), *small)
    data = lax.all_to_all(data, "view", 0, 0, tiled=True)
    matrices = jax.ShapeDtypeStruct((views, lanes, 2 * lanes), jnp.bfloat16)

    block = (wide, COLS, lanes)
    strips = [(halo, COLS, lanes)] * (ITERS - 1) + [(halo // 2, COLS, lanes)]
    scratch = [
        pltpu.VMEM((views, wide, cols, lanes), jnp.float32),
        pltpu.VMEM((views, rows * cols, lanes), jnp.float32),
    ]

    def joined(part, near, far, count):
        shapes = [(count, width, lanes) for width in (COLS, 8, 8)]
        total, yn, yf = call(rows_kernel, (flags, part, near, far), shapes)
        yn, yf = swapped(yn, yf, "view")
        return total, yn, yf

    yn, yf = swapped(estimate, estimate, "view")
    thin = (halo // 2, COLS, lanes)
    own, near, far = call(
        functools.partial(columns_kernel, ns // 2),
        (flags, estimate, yn, yf),
        ((rows, COLS, lanes), thin, thin),
    )
    near, far = swapped(near, far, "tile")
    current, part, near, far, conv, corr, table = call(
        functools.partial(first_kernel, sizes),
        (flags, own, near, far, data),
        (block, block, strips[0], strips[0], matrices, matrices, (views, 16, lanes)),
        scratch + [pltpu.VMEM((2 * views, lanes), jnp.float32)],
        limit=16 << 20,
    )
    for step in range(1, ITERS):
        near, far = swapped(near, far, "tile")
        total, yn, yf = joined(part, near, far, wide)
        current, part, near, far = call(
            functools.partial(pass_kernel, sizes, views),
            (flags, current, total, yn, yf, data, conv, corr, table),
            (block, block, strips[step], strips[step]),
            scratch,
            limit=12 << 20,
        )
    near, far = swapped(near, far, "tile")
    total, yn, yf = joined(part, near, far, rows)
    (out,) = call(
        functools.partial(final_kernel, views, nf // 2, ns // 2),
        (flags, current, total, yn, yf),
        ((rows, cols, lanes),),
        [pltpu.VMEM((rows, COLS, lanes), jnp.float32)],
    )
    return out


def solution(mesh):
    in_specs = (
        P("tile", "view", None),
        P("view", "tile", None, None),
        P("view", None),
        P("view", None),
        P("view", None),
    )
    out_specs = P("tile", "view", None)
    return jax.shard_map(local, mesh=mesh, in_specs=in_specs, out_specs=out_specs, check_vma=False)
```
